32 devices in a mesh: pa: 1, row: 32 (over z, y, x, core).
Axes of the slice: x: 2, y: 2, z: 4, core: 2. Of those that a mesh axis runs over, the one named last changes fastest.
Arguments:
- raw_pulses: bfloat16 [64, 2, 16384], P(('pa', 'row')), may hold values from -6 to 6
- chirp_taps: bfloat16 [2, 512], replicated, may hold values from -0.1875 to 0.1875
- steer_angle: float32 [1, 64, 64], P('pa'), may hold values from -3.140625 to 3.140625
- interp_weights: bfloat16 [4, 1, 64, 128], P(None, 'pa', None, 'row'), may hold values from -3 to 3
- tile_phase: bfloat16 [1, 64, 128], P('pa', None, 'row'), may hold values from -3.140625 to 3.140625
- tap_offset: int32 [1, 64, 128], P('pa', None, 'row'), may hold values from -3 to 2
- image_slot: int32 [1, 64, 128], P('pa', None, 'row'), may hold values from 0 to 63
- tile_owner: int32 [1, 64, 128], P('pa', None, 'row'), may hold values from 0 to 31, as said below
Outputs:
- image: float32 [32, 64, 2, 128], P('row', 'pa')
The draws below stay inside these ranges and needn't reach their ends.
Inputs may be any that keep to these rules, and one draw needn't show every extreme that they name: `tile_owner`: among the tiles of one device (1 subapertures, all beams and 4 range tiles at one index of pa and of row) no owner is named more than 16 times; in every draw one owner, the same for all devices, is named exactly 16 times by the tiles of every device.
All inputs are finite; a program needn't handle non-finite values.
Results may differ from the reference program's by a relative error of at most 0.0085.
Values may be sent and summed in bfloat16 or wider, within the bound.
A program may use at most 64 MiB of HBM per device.

```python
import jax
import jax.numpy as jnp
from jax import lax

R = 16384
TAPS = 512
A = 64
BEAMS = 64
TILE = 128
IMG_ROWS = 64
OWNERS = 32
GROUPS = 1
P_SIZE = 64
NSUB = 1
NRT = 128
SUB_DEV = 1
RT_DEV = 4
TILES_DEV = 256
CAP = 16
FAN = 4


def draw_tile_owner(key, part):
    heavy_owner = jax.random.randint(jax.random.fold_in(key, 11), (), 0, OWNERS)
    block_keys = jax.random.split(jax.random.fold_in(key, 12), GROUPS * OWNERS)

    def one_block(block_key):
        key_one, key_two = jax.random.split(block_key)
        scattered = jax.random.permutation(key_one, (OWNERS - 1) * CAP)[:TILES_DEV - CAP] // CAP
        scattered = (scattered + (scattered >= heavy_owner).astype(jnp.int32)).astype(jnp.int32)
        listed = jnp.concatenate([jnp.full((CAP,), heavy_owner, jnp.int32), scattered])
        return listed[jax.random.permutation(key_two, TILES_DEV)]
    blocks = jax.vmap(one_block)(block_keys)
    blocks = blocks.reshape(GROUPS, OWNERS, SUB_DEV, BEAMS, RT_DEV)
    return blocks.transpose(0, 2, 3, 1, 4).reshape(NSUB, BEAMS, NRT).astype(jnp.int32)


def set_ends(entries, rng, low, top_value):
    index_at = [jax.random.randint(jax.random.fold_in(rng, axis), (), 0, length) for axis, length in enumerate(entries.shape)]
    main_axis = entries.shape.index(max(entries.shape))
    next_to = index_at[:main_axis] + [(index_at[main_axis] + 1) % entries.shape[main_axis]] + index_at[main_axis + 1:]
    return entries.at[tuple(index_at)].set(low).at[tuple(next_to)].set(top_value)


def steps_of(rng, shape, cuts, smallest, largest):
    loudness, own = 1.0, jax.random.fold_in(rng, 6)
    for dim, blocks in cuts:
        draws = jnp.exp(jax.random.uniform(jax.random.fold_in(own, dim), (blocks,), jnp.float32, smallest / len(cuts), largest / len(cuts)))
        loudness = loudness * jnp.repeat(draws, shape[dim] // blocks).reshape([-1 if axis == dim else 1 for axis in range(len(shape))])
    return loudness


def centred(rng, dims, width, most, pieces=(), held_as=jnp.bfloat16):
    level = steps_of(rng, dims, pieces, -0.22, 0.18) if pieces else 1.0
    values = jax.random.normal(rng, dims, jnp.float32) * width * level
    return jnp.minimum(jnp.maximum(values, -most), most).astype(held_as)


def setup_inputs(seed: int = 0) -> dict:
    keys = jax.random.split(jax.random.key(seed), 9)
    return {
        "raw_pulses": centred(keys[0], (P_SIZE, 2, R), 1.0, 6.0, ((0, 32),)),
        "chirp_taps": centred(keys[1], (2, TAPS), (2 * TAPS) ** -0.5, 0.1875),
        "steer_angle": jnp.clip(jax.random.uniform(keys[2], (NSUB, A, BEAMS), jnp.float32, -3.140625, 3.140625), -3.140625, 3.140625),
        "interp_weights": centred(keys[3], (4, NSUB, BEAMS, NRT), 0.5, 3.0, ((3, 32),)),
        "tile_phase": jnp.clip(jax.random.uniform(keys[4], (NSUB, BEAMS, NRT), jnp.float32, -3.140625, 3.140625), -3.140625, 3.140625).astype(jnp.bfloat16),
        "tap_offset": set_ends(jax.random.randint(keys[5], (NSUB, BEAMS, NRT), -3, 3), jax.random.fold_in(keys[5], 1), -3, 2).astype(jnp.int32),
        "image_slot": set_ends(jax.random.randint(keys[6], (NSUB, BEAMS, NRT), 0, IMG_ROWS), jax.random.fold_in(keys[6], 1), 0, IMG_ROWS - 1).astype(jnp.int32),
        "tile_owner": draw_tile_owner(jax.random.fold_in(keys[8], 71), 0),
    }


def band_of(taps):
    extended = jnp.concatenate([taps, jnp.zeros((TAPS + 1,), taps.dtype)])
    repeated = jnp.tile(extended, TAPS)[: 2 * TAPS * TAPS]
    return repeated.reshape(TAPS, 2 * TAPS).T


def toeplitz_matrix(chirp_taps):
    real_taps = band_of(chirp_taps[0])
    imag_taps = band_of(chirp_taps[1])
    upper = jnp.concatenate([real_taps, -imag_taps], 1)
    lower = jnp.concatenate([imag_taps, real_taps], 1)
    return jnp.concatenate([upper, lower], 0)


def compress(pulses, matrix):
    count_pulses = pulses.shape[0]
    length = pulses.shape[2]
    block_count = length // TAPS
    padded = jnp.pad(pulses, ((0, 0), (0, 0), (0, TAPS)))
    front_half = padded[:, :, :length].reshape(count_pulses, 2, block_count, TAPS)
    back_half = padded[:, :, TAPS:].reshape(count_pulses, 2, block_count, TAPS)
    extended = jnp.concatenate([front_half, back_half], 3)
    extended = extended.transpose(0, 2, 1, 3).reshape(count_pulses * block_count, 4 * TAPS)
    product = jnp.dot(extended, matrix, preferred_element_type=jnp.float32)
    product = product.reshape(count_pulses, block_count, 2, TAPS).transpose(0, 2, 1, 3)
    return product.reshape(count_pulses, 2, length).astype(jnp.bfloat16)


def beamform(grouped, angles):
    steering = jnp.concatenate([jnp.cos(angles), jnp.sin(angles)], 2).astype(jnp.bfloat16)
    steering = steering.astype(jnp.float32)
    from_real = jnp.einsum("sac,sar->scr", steering, grouped[:, :, 0].astype(jnp.float32))
    from_imag = jnp.einsum("sac,sar->scr", steering, grouped[:, :, 1].astype(jnp.float32))
    beam_count = angles.shape[2]
    beam_real = from_real[:, :beam_count] - from_imag[:, beam_count:]
    beam_imag = from_imag[:, :beam_count] + from_real[:, beam_count:]
    norm_factor = angles.shape[1] ** -0.5
    return (jnp.stack([beam_real, beam_imag], 2) * norm_factor).astype(jnp.bfloat16)


def interpolate(beam_tiles, weights, phases, offsets):
    padded = jnp.pad(beam_tiles.astype(jnp.float32), ((0, 0), (0, 0), (4, 4)))
    shift_values = jnp.arange(-4, 5, dtype=jnp.int32)
    tap_index = jnp.arange(4, dtype=jnp.int32)
    matches = (offsets[:, None, None] + tap_index[None, None, :] - 1) == shift_values[None, :, None]
    band_coeffs = jnp.sum(jnp.where(matches, weights.astype(jnp.float32)[:, None, :], 0.0), 2)
    summed_taps = band_coeffs[:, 0, None, None] * padded[:, :, 0:TILE]
    for position in range(1, 9):
        summed_taps = summed_taps + band_coeffs[:, position, None, None] * padded[:, :, position:position + TILE]
    cosine = jnp.cos(phases.astype(jnp.float32))[:, None]
    sine_part = jnp.sin(phases.astype(jnp.float32))[:, None]
    out_real = cosine * summed_taps[:, 0] - sine_part * summed_taps[:, 1]
    out_imag = sine_part * summed_taps[:, 0] + cosine * summed_taps[:, 1]
    return jnp.stack([out_real, out_imag], 1).astype(jnp.bfloat16)


def reference(raw_pulses, chirp_taps, steer_angle, interp_weights, tile_phase, tap_offset, image_slot, tile_owner):
    matrix = toeplitz_matrix(chirp_taps)

    def one_subaperture(image_sum, sub_index):
        pulses = lax.dynamic_slice_in_dim(raw_pulses, sub_index * A, A, 0)
        compressed = compress(pulses, matrix)
        formed = beamform(compressed[None], steer_angle[sub_index][None])[0]
        beam_tiles = formed.reshape(BEAMS, 2, NRT, TILE).transpose(0, 2, 1, 3).reshape(BEAMS * NRT, 2, TILE)
        weights = interp_weights[:, sub_index].reshape(4, BEAMS * NRT).T
        phases = tile_phase[sub_index].reshape(BEAMS * NRT)
        offsets = tap_offset[sub_index].reshape(BEAMS * NRT)
        targets = tile_owner[sub_index].reshape(BEAMS * NRT) * IMG_ROWS + image_slot[sub_index].reshape(BEAMS * NRT)
        shifted = interpolate(beam_tiles, weights, phases, offsets)
        flat_tiles = shifted.reshape(BEAMS * NRT, 2 * TILE).astype(jnp.float32)
        image_sum = image_sum + jax.ops.segment_sum(flat_tiles, targets, OWNERS * IMG_ROWS)
        return image_sum, None

    start_image = jnp.zeros((OWNERS * IMG_ROWS, 2 * TILE), jnp.float32)
    image_sum, unused_out = lax.scan(one_subaperture, start_image, jnp.arange(NSUB, dtype=jnp.int32))
    return (image_sum * (float(FAN) ** -0.5)).reshape(OWNERS, IMG_ROWS, 2, TILE)
```

```python
import functools

import jax
import jax.numpy as jnp
from jax import lax
from jax.experimental import pallas as pl
from jax.experimental.pallas import tpu as pltpu
from jax.sharding import PartitionSpec as P

LANES = 128
IMG_ROWS = 64
F32 = jnp.float32
BF16 = jnp.bfloat16
NT = (((1,), (1,)), ((), ()))
TN = (((0,), (0,)), ((), ()))
WEIGHTS = 4
PLANE = 8


def iota(shape, dim):
    return lax.broadcasted_iota(jnp.int32, shape, dim)


def one_hot(cond):
    return jnp.where(cond, 1.0, 0.0)


def mirrored(me, n, i):
    if n & (n - 1):
        return lax.rem(me + i, n)
    return jnp.bitwise_xor(me, n - i)


def body(
    n,
    rows_out,
    scale,
    x_hbm,
    taps_hbm,
    angle_hbm,
    owner_hbm,
    slot_hbm,
    weight_hbm,
    phase_hbm,
    offset_hbm,
    out_ref,
    x_ref,
    taps_ref,
    angle_ref,
    owner_ref,
    slot_ref,
    weight_ref,
    phase_ref,
    offset_ref,
    xs,
    send_one,
    recv_one,
    send_slot,
    recv_slot,
    send_two,
    recv_two,
    steer,
    packed,
    coeff,
    turn,
    pack,
    sems,
    load_sems,
):
    me = lax.axis_index("row")
    pulses, _, length = x_ref.shape
    blocks = length // LANES
    reach = taps_ref.shape[1] // LANES
    group = 2 * blocks // n
    width = pulses * group
    tiles = group // 2
    count_a, count_beams = angle_ref.shape
    count_tiles = tiles * count_beams
    capacity = send_two.shape[1]
    chunk = PLANE if n % PLANE == 0 else n

    given = (x_hbm, taps_hbm, angle_hbm, owner_hbm, slot_hbm, weight_hbm, phase_hbm, offset_hbm)
    held = (x_ref, taps_ref, angle_ref, owner_ref, slot_ref, weight_ref, phase_ref, offset_ref)
    held_copies = [
        pltpu.make_async_copy(source, target, load_sems.at[index])
        for index, (source, target) in enumerate(zip(given, held))
    ]
    barrier = pltpu.get_barrier_semaphore()

    def greet(i, carry):
        pl.semaphore_signal(barrier, inc=1, device_id={"row": lax.rem(me + i, n)})
        return carry

    lax.fori_loop(1, n, greet, 0)
    for copy in held_copies:
        copy.start()

    held_copies[0].wait()
    for p in range(pulses):
        for b in range(blocks):
            piece = x_ref[p, :, b * LANES : (b + 1) * LANES]
            xs[p, 2 * b : 2 * b + 2, :] = piece.astype(F32)
        xs[p, 2 * blocks :, :] = jnp.zeros((2 * reach, LANES), F32)
    keep = iota((LANES, LANES), 1) >= iota((LANES, LANES), 0)
    zero = jnp.zeros((LANES, LANES), F32)
    held_copies[1].wait()
    halves = []
    for c in range(2):
        rolled = []
        for j in range(reach):
            row = taps_ref[c : c + 1, j * LANES : (j + 1) * LANES].astype(F32)
            row = jnp.broadcast_to(row, (LANES, LANES))
            rolled.append(pltpu.roll(row, 0, 1, stride=1, stride_axis=0))
        rolled = [zero] + rolled + [zero]
        halves.append(
            jnp.concatenate(
                [jnp.where(keep, rolled[j + 1], rolled[j]).astype(BF16) for j in range(reach + 1)], 1
            )
        )
    band = jnp.concatenate(halves, 0)
    outs = []
    parity = iota((2 * blocks, LANES), 0) % 2 == 0
    for p in range(pulses):
        window = jnp.concatenate(
            [xs[p, 2 * j : 2 * j + 2 * blocks, :].astype(BF16) for j in range(reach + 1)], 1
        )
        product = lax.dot_general(window, band, NT, preferred_element_type=F32)
        first, second = product[:, :LANES], product[:, LANES:]
        crossed = jnp.where(
            parity, pltpu.roll(second, 2 * blocks - 1, 0), -pltpu.roll(second, 1, 0)
        )
        outs.append((first + crossed).reshape(n, group, LANES))
    send_one[...] = jnp.concatenate(outs, 1).astype(BF16)

    pl.semaphore_wait(barrier, n - 1)

    def push(source, target, send_sem, recv_sem, to):
        pltpu.make_async_remote_copy(
            src_ref=source.at[to],
            dst_ref=target.at[me],
            send_sem=send_sem,
            recv_sem=recv_sem,
            device_id={"row": to},
        ).start()

    def keep_own(source, target, recv_sem):
        pltpu.make_async_copy(source.at[me], target.at[me], recv_sem).start()

    def exchange(source, target, send_sem, recv_sem):
        def first(i, carry):
            @pl.when(i != me)
            def _():
                push(source, target, send_sem, recv_sem, i)

            return carry

        def rest(i, carry):
            to = mirrored(me, n, i)

            @pl.when(to >= 2)
            def _():
                push(source, target, send_sem, recv_sem, to)

            return carry

        lax.fori_loop(0, 2, first, 0)
        lax.fori_loop(1, n, rest, 0)
        keep_own(source, target, recv_sem)

    def arrived(target, recv_sem):
        pltpu.make_async_copy(target, target, recv_sem).wait()

    def departed(source, send_sem):
        part = source.at[pl.ds(0, n - 1)]
        pltpu.make_async_copy(part, part, send_sem).wait()

    exchange(send_one, recv_one, sems.at[0], sems.at[1])

    held_copies[3].wait()
    held_copies[4].wait()
    owner = jnp.concatenate([owner_ref[t : t + 1, :] for t in range(tiles)], 1)
    slot = jnp.concatenate([slot_ref[t : t + 1, :] for t in range(tiles)], 1)
    member = one_hot(owner == iota((n, count_tiles), 0))
    before = one_hot(iota((count_tiles, count_tiles), 0) < iota((count_tiles, count_tiles), 1))
    ahead = jnp.dot(member.astype(BF16), before.astype(BF16), preferred_element_type=F32)
    rank = jnp.sum(ahead * member, 0, keepdims=True).astype(jnp.int32)
    ranked = jnp.where(rank == iota((LANES, count_tiles), 0), slot.astype(F32), 0.0)
    slots = lax.dot_general(
        member.astype(BF16), ranked.astype(BF16), NT, preferred_element_type=F32
    )
    send_slot[...] = slots.reshape(n, 1, LANES)
    exchange(send_slot, recv_slot, sems.at[2], sems.at[3])
    place = owner * capacity + rank
    pack[...] = one_hot(place == iota((n * capacity, count_tiles), 0)).astype(BF16)

    for index in (2, 5, 6, 7):
        held_copies[index].wait()
    weights = weight_ref[...].astype(F32)
    offsets = offset_ref[...].astype(F32)
    table = [
        jnp.concatenate([weights[k, t : t + 1, :] for t in range(tiles)], 1) for k in range(WEIGHTS)
    ]
    table.append(jnp.concatenate([offsets[t : t + 1, :] for t in range(tiles)], 1))
    table.append(jnp.zeros((16 - len(table), count_tiles), F32))
    table = jnp.concatenate(table, 0).astype(BF16)
    columns = lax.dot_general(pack[...], table, NT, preferred_element_type=F32)
    rows = chunk * capacity
    lane = iota((n * capacity, LANES), 1)
    offset = jnp.broadcast_to(columns[:, WEIGHTS : WEIGHTS + 1], (n * capacity, LANES))
    offset = offset.astype(jnp.int32)
    turn[...] = (2 - offset).reshape(n // chunk, rows, LANES)
    for k in range(WEIGHTS):
        reached = lane + offset + (k - 1)
        inside = (reached >= 0) & (reached < LANES)
        level = jnp.where(inside, columns[:, k : k + 1], 0.0)
        coeff[:, k] = level.reshape(n // chunk, rows, LANES)

    span = n * width
    pulse_of = iota((count_a, span), 1) // group == iota((count_a, span), 0)
    expand = one_hot(pulse_of).astype(BF16)
    angles = angle_ref[...]
    cosine = lax.dot_general(
        jnp.cos(angles).astype(BF16), expand, TN, preferred_element_type=F32
    )
    sine = lax.dot_general(
        jnp.sin(angles).astype(BF16), expand, TN, preferred_element_type=F32
    )
    phases = phase_ref[...].astype(F32)
    spare = jnp.zeros((LANES - 2 * tiles, count_beams), F32)
    norm = count_a ** (-0.5)
    turns = jnp.concatenate([norm * jnp.cos(phases), norm * jnp.sin(phases), spare], 0).T
    column = iota((count_beams, span), 1) % group
    even = column % 2 == 0
    along = jnp.where(even, cosine, -sine)
    across = jnp.where(even, sine, cosine)
    for t in range(tiles):
        here = column // 2 == t
        c = turns[:, t : t + 1]
        s = turns[:, tiles + t : tiles + t + 1]
        base = t * count_beams
        steer[base : base + count_beams, :span] = jnp.where(
            here, c * along - s * across, 0.0
        ).astype(BF16)
        steer[base : base + count_beams, span:] = jnp.where(
            here, s * along + c * across, 0.0
        ).astype(BF16)
    for j in range(n // chunk):
        part = jnp.dot(
            pack[j * rows : (j + 1) * rows, :], steer[...], preferred_element_type=F32
        ).astype(BF16)
        packed[j, :rows, :] = part[:, :span]
        packed[j, rows:, :] = part[:, span:]

    arrived(recv_one, sems.at[1])
    turned = recv_one[...].reshape(span, LANES)
    for step in range(n // chunk):
        j = lax.rem(lax.div(me, chunk) + 1 + step, n // chunk)
        formed = jnp.dot(packed[j], turned, preferred_element_type=F32)
        by = turn[j]
        one, two, four = by % 2 == 1, by // 2 % 2 == 1, by >= 4
        taps = [coeff[j, k] for k in range(WEIGHTS)]
        shifted = []
        for c in range(2):
            x = formed[c * rows : (c + 1) * rows]
            x = jnp.where(one, x, pltpu.roll(x, LANES - 1, 1))
            x = jnp.where(two, pltpu.roll(x, 2, 1), x)
            x = jnp.where(four, pltpu.roll(x, 4, 1), x)
            total = taps[0] * x
            for k in range(1, WEIGHTS):
                total = total + taps[k] * pltpu.roll(x, LANES - k, 1)
            shifted.append(total)
        ready = jnp.concatenate(shifted, 1).astype(BF16)
        send_two[pl.ds(j * chunk, chunk)] = ready.reshape(chunk, capacity, 2 * LANES)

        def give(i, carry):
            to = j * chunk + lax.rem(me + 1 + i, chunk)

            @pl.when(to != me)
            def _():
                push(send_two, recv_two, sems.at[4], sems.at[5], to)

            return carry

        lax.fori_loop(0, chunk, give, 0)
    keep_own(send_two, recv_two, sems.at[5])

    arrived(recv_slot, sems.at[3])
    total_slots = n * capacity
    got = recv_slot[...].reshape(n, LANES).astype(BF16)
    source_of = iota((total_slots, n), 0) // capacity == iota((total_slots, n), 1)
    got = jnp.dot(one_hot(source_of).astype(BF16), got, preferred_element_type=F32)
    wanted = iota((total_slots, LANES), 0) % capacity == iota((total_slots, LANES), 1)
    got = jnp.sum(jnp.where(wanted, got, 0.0), 1, keepdims=True).astype(jnp.int32)
    select = one_hot(got == iota((total_slots, LANES), 1)).T[:rows_out].astype(BF16)
    arrived(recv_two, sems.at[5])
    landed = recv_two[...].reshape(total_slots, 2 * LANES)
    image = jnp.dot(select, landed, preferred_element_type=F32) * scale
    out_ref[:, 0, :] = image[:, :LANES]
    out_ref[:, 1, :] = image[:, LANES:]
    departed(send_one, sems.at[0])
    departed(send_slot, sems.at[2])
    departed(send_two, sems.at[4])


def per_device(
    n,
    pa,
    raw_pulses,
    chirp_taps,
    steer_angle,
    interp_weights,
    tile_phase,
    tap_offset,
    image_slot,
    tile_owner,
):
    pulses, _, length = raw_pulses.shape
    _, count_a, count_beams = steer_angle.shape
    tiles = tile_owner.shape[2]
    count_tiles = count_beams * tiles
    capacity = 2 * count_tiles // n
    chunk = PLANE if n % PLANE == 0 else n
    blocks = length // LANES
    width = pulses * 2 * blocks // n
    reach = chirp_taps.shape[1] // LANES
    spread_factor = float(pa * count_tiles // IMG_ROWS) ** (-0.5)
    operands = (
        raw_pulses,
        chirp_taps,
        steer_angle.reshape(count_a, count_beams),
        tile_owner.transpose(0, 2, 1).reshape(tiles, count_beams),
        image_slot.transpose(0, 2, 1).reshape(tiles, count_beams),
        interp_weights.transpose(0, 1, 3, 2).reshape(4, tiles, count_beams),
        tile_phase.transpose(0, 2, 1).reshape(tiles, count_beams),
        tap_offset.transpose(0, 2, 1).reshape(tiles, count_beams),
    )
    image_part = pl.pallas_call(
        functools.partial(body, n, IMG_ROWS, spread_factor),
        out_shape=pltpu.VMEM((IMG_ROWS, 2, LANES), F32),
        in_specs=[pl.BlockSpec(memory_space=pltpu.HBM)] * len(operands),
        out_specs=pl.BlockSpec(memory_space=pltpu.VMEM),
        scratch_shapes=[pltpu.VMEM(x.shape, x.dtype) for x in operands]
        + [
            pltpu.VMEM((pulses, 2 * blocks + 2 * reach, LANES), F32),
            pltpu.VMEM((n, width, LANES), BF16),
            pltpu.VMEM((n, width, LANES), BF16),
            pltpu.VMEM((n, 1, LANES), F32),
            pltpu.VMEM((n, 1, LANES), F32),
            pltpu.VMEM((n, capacity, 2 * LANES), BF16),
            pltpu.VMEM((n, capacity, 2 * LANES), BF16),
            pltpu.VMEM((count_tiles, 2 * n * width), BF16),
            pltpu.VMEM((n // chunk, 2 * chunk * capacity, n * width), BF16),
            pltpu.VMEM((n // chunk, WEIGHTS, chunk * capacity, LANES), F32),
            pltpu.VMEM((n // chunk, chunk * capacity, LANES), jnp.int32),
            pltpu.VMEM((n * capacity, count_tiles), BF16),
            pltpu.SemaphoreType.DMA((6,)),
            pltpu.SemaphoreType.DMA((len(operands),)),
        ],
        compiler_params=pltpu.CompilerParams(
            collective_id=0, has_side_effects=True, vmem_limit_bytes=62 << 20
        ),
    )(*operands)
    if pa > 1:
        image_part = lax.psum_scatter(image_part, "pa", scatter_dimension=0, tiled=True)
    return image_part[None]


def solution(mesh):
    placed = (
        P(("pa", "row"), None, None),
        P(),
        P("pa", None, None),
        P(None, "pa", None, "row"),
        P("pa", None, "row"),
        P("pa", None, "row"),
        P("pa", None, "row"),
        P("pa", None, "row"),
    )
    return jax.shard_map(
        functools.partial(per_device, mesh.shape["row"], mesh.shape["pa"]),
        mesh=mesh,
        in_specs=placed,
        out_specs=P("row", "pa", None, None),
        check_vma=False,
    )
```

```python
import functools

import jax
import jax.numpy as jnp
from jax import lax
from jax.experimental import pallas as pl
from jax.experimental.pallas import tpu as pltpu
from jax.sharding import PartitionSpec as P

LANES = 128
IMG_ROWS = 64
F32 = jnp.float32
BF16 = jnp.bfloat16
NT = (((1,), (1,)), ((), ()))
TN = (((0,), (0,)), ((), ()))
WEIGHTS = 4
PLANE = 8


def iota(shape, dim):
    return lax.broadcasted_iota(jnp.int32, shape, dim)


def one_hot(cond):
    return jnp.where(cond, 1.0, 0.0)


def mirrored(me, n, i):
    if n & (n - 1):
        return lax.rem(me + i, n)
    return jnp.bitwise_xor(me, n - i)


def body(
    n,
    rows_out,
    scale,
    x_hbm,
    taps_hbm,
    angle_hbm,
    owner_hbm,
    slot_hbm,
    weight_hbm,
    phase_hbm,
    offset_hbm,
    out_ref,
    x_ref,
    taps_ref,
    angle_ref,
    owner_ref,
    slot_ref,
    weight_ref,
    phase_ref,
    offset_ref,
    xs,
    send_one,
    recv_one,
    send_slot,
    recv_slot,
    send_two,
    recv_two,
    steer,
    packed,
    coeff,
    turn,
    pack,
    sems,
    load_sems,
):
    me = lax.axis_index("row")
    pulses, _, length = x_ref.shape
    blocks = length // LANES
    reach = taps_ref.shape[1] // LANES
    group = 2 * blocks // n
    width = pulses * group
    tiles = group // 2
    count_a, count_beams = angle_ref.shape
    count_tiles = tiles * count_beams
    capacity = send_two.shape[1]
    chunk = PLANE if n % PLANE == 0 else n

    given = (x_hbm, taps_hbm, angle_hbm, owner_hbm, slot_hbm, weight_hbm, phase_hbm, offset_hbm)
    held = (x_ref, taps_ref, angle_ref, owner_ref, slot_ref, weight_ref, phase_ref, offset_ref)
    held_copies = [
        pltpu.make_async_copy(source, target, load_sems.at[index])
        for index, (source, target) in enumerate(zip(given, held))
    ]
    barrier = pltpu.get_barrier_semaphore()

    def greet(i, carry):
        pl.semaphore_signal(barrier, inc=1, device_id={"row": lax.rem(me + i, n)})
        return carry

    lax.fori_loop(1, n, greet, 0)
    for copy in held_copies:
        copy.start()

    held_copies[0].wait()
    for p in range(pulses):
        for b in range(blocks):
            piece = x_ref[p, :, b * LANES : (b + 1) * LANES]
            xs[p, 2 * b : 2 * b + 2, :] = piece.astype(F32)
        xs[p, 2 * blocks :, :] = jnp.zeros((2 * reach, LANES), F32)
    keep = iota((LANES, LANES), 1) >= iota((LANES, LANES), 0)
    zero = jnp.zeros((LANES, LANES), F32)
    held_copies[1].wait()
    halves = []
    for c in range(2):
        rolled = []
        for j in range(reach):
            row = taps_ref[c : c + 1, j * LANES : (j + 1) * LANES].astype(F32)
            row = jnp.broadcast_to(row, (LANES, LANES))
            rolled.append(pltpu.roll(row, 0, 1, stride=1, stride_axis=0))
        rolled = [zero] + rolled + [zero]
        halves.append(
            jnp.concatenate(
                [jnp.where(keep, rolled[j + 1], rolled[j]).astype(BF16) for j in range(reach + 1)], 1
            )
        )
    band = jnp.concatenate(halves, 0)
    outs = []
    parity = iota((2 * blocks, LANES), 0) % 2 == 0
    for p in range(pulses):
        window = jnp.concatenate(
            [xs[p, 2 * j : 2 * j + 2 * blocks, :].astype(BF16) for j in range(reach + 1)], 1
        )
        product = lax.dot_general(window, band, NT, preferred_element_type=F32)
        first, second = product[:, :LANES], product[:, LANES:]
        crossed = jnp.where(
            parity, pltpu.roll(second, 2 * blocks - 1, 0), -pltpu.roll(second, 1, 0)
        )
        outs.append((first + crossed).reshape(n, group, LANES))
    send_one[...] = jnp.concatenate(outs, 1).astype(BF16)

    pl.semaphore_wait(barrier, n - 1)

    def push(source, target, send_sem, recv_sem, to):
        pltpu.make_async_remote_copy(
            src_ref=source.at[to],
            dst_ref=target.at[me],
            send_sem=send_sem,
            recv_sem=recv_sem,
            device_id={"row": to},
        ).start()

    def keep_own(source, target, recv_sem):
        pltpu.make_async_copy(source.at[me], target.at[me], recv_sem).start()

    def exchange(source, target, send_sem, recv_sem):
        def first(i, carry):
            @pl.when(i != me)
            def _():
                push(source, target, send_sem, recv_sem, i)

            return carry

        def rest(i, carry):
            to = mirrored(me, n, i)

            @pl.when(to >= 2)
            def _():
                push(source, target, send_sem, recv_sem, to)

            return carry

        lax.fori_loop(0, 2, first, 0)
        lax.fori_loop(1, n, rest, 0)
        keep_own(source, target, recv_sem)

    def arrived(target, recv_sem):
        pltpu.make_async_copy(target, target, recv_sem).wait()

    def departed(source, send_sem):
        part = source.at[pl.ds(0, n - 1)]
        pltpu.make_async_copy(part, part, send_sem).wait()

    exchange(send_one, recv_one, sems.at[0], sems.at[1])

    held_copies[3].wait()
    held_copies[4].wait()
    owner = jnp.concatenate([owner_ref[t : t + 1, :] for t in range(tiles)], 1)
    slot = jnp.concatenate([slot_ref[t : t + 1, :] for t in range(tiles)], 1)
    member = one_hot(owner == iota((n, count_tiles), 0))
    before = one_hot(iota((count_tiles, count_tiles), 0) < iota((count_tiles, count_tiles), 1))
    ahead = jnp.dot(member.astype(BF16), before.astype(BF16), preferred_element_type=F32)
    rank = jnp.sum(ahead * member, 0, keepdims=True).astype(jnp.int32)
    ranked = jnp.where(rank == iota((LANES, count_tiles), 0), slot.astype(F32), 0.0)
    slots = lax.dot_general(
        member.astype(BF16), ranked.astype(BF16), NT, preferred_element_type=F32
    )
    send_slot[...] = slots.reshape(n, 1, LANES)
    exchange(send_slot, recv_slot, sems.at[2], sems.at[3])
    place = owner * capacity + rank
    pack[...] = one_hot(place == iota((n * capacity, count_tiles), 0)).astype(BF16)

    for index in (2, 5, 6, 7):
        held_copies[index].wait()
    weights = weight_ref[...].astype(F32)
    offsets = offset_ref[...].astype(F32)
    table = [
        jnp.concatenate([weights[k, t : t + 1, :] for t in range(tiles)], 1) for k in range(WEIGHTS)
    ]
    table.append(jnp.concatenate([offsets[t : t + 1, :] for t in range(tiles)], 1))
    table.append(jnp.zeros((16 - len(table), count_tiles), F32))
    table = jnp.concatenate(table, 0).astype(BF16)
    columns = lax.dot_general(pack[...], table, NT, preferred_element_type=F32)
    rows = chunk * capacity
    lane = iota((n * capacity, LANES), 1)
    offset = jnp.broadcast_to(columns[:, WEIGHTS : WEIGHTS + 1], (n * capacity, LANES))
    offset = offset.astype(jnp.int32)
    turn[...] = (2 - offset).reshape(n // chunk, rows, LANES)
    for k in range(WEIGHTS):
        reached = lane + offset + (k - 1)
        inside = (reached >= 0) & (reached < LANES)
        level = jnp.where(inside, columns[:, k : k + 1], 0.0)
        coeff[:, k] = level.reshape(n // chunk, rows, LANES)

    span = n * width
    pulse_of = iota((count_a, span), 1) // group == iota((count_a, span), 0)
    expand = one_hot(pulse_of).astype(BF16)
    angles = angle_ref[...]
    cosine = lax.dot_general(
        jnp.cos(angles).astype(BF16), expand, TN, preferred_element_type=F32
    )
    sine = lax.dot_general(
        jnp.sin(angles).astype(BF16), expand, TN, preferred_element_type=F32
    )
    phases = phase_ref[...].astype(F32)
    spare = jnp.zeros((LANES - 2 * tiles, count_beams), F32)
    norm = count_a ** (-0.5)
    turns = jnp.concatenate([norm * jnp.cos(phases), norm * jnp.sin(phases), spare], 0).T
    column = iota((count_beams, span), 1) % group
    even = column % 2 == 0
    along = jnp.where(even, cosine, -sine)
    across = jnp.where(even, sine, cosine)
    for t in range(tiles):
        here = column // 2 == t
        c = turns[:, t : t + 1]
        s = turns[:, tiles + t : tiles + t + 1]
        base = t * count_beams
        steer[base : base + count_beams, :span] = jnp.where(
            here, c * along - s * across, 0.0
        ).astype(BF16)
        steer[base : base + count_beams, span:] = jnp.where(
            here, s * along + c * across, 0.0
        ).astype(BF16)
    for j in range(n // chunk):
        part = jnp.dot(
            pack[j * rows : (j + 1) * rows, :], steer[...], preferred_element_type=F32
        ).astype(BF16)
        packed[j, :rows, :] = part[:, :span]
        packed[j, rows:, :] = part[:, span:]

    arrived(recv_one, sems.at[1])
    turned = recv_one[...].reshape(span, LANES)
    half = n // chunk // 2
    near, far = list(range(half)), list(range(n // chunk - 1, half - 1, -1))
    for low, high in zip(far + near, near + far):
        j = jnp.where(me < half * chunk, low, high)
        formed = jnp.dot(packed[j], turned, preferred_element_type=F32)
        by = turn[j]
        one, two, four = by % 2 == 1, by // 2 % 2 == 1, by >= 4
        taps = [coeff[j, k] for k in range(WEIGHTS)]
        shifted = []
        for c in range(2):
            x = formed[c * rows : (c + 1) * rows]
            x = jnp.where(one, x, pltpu.roll(x, LANES - 1, 1))
            x = jnp.where(two, pltpu.roll(x, 2, 1), x)
            x = jnp.where(four, pltpu.roll(x, 4, 1), x)
            total = taps[0] * x
            for k in range(1, WEIGHTS):
                total = total + taps[k] * pltpu.roll(x, LANES - k, 1)
            shifted.append(total)
        ready = jnp.concatenate(shifted, 1).astype(BF16)
        send_two[pl.ds(j * chunk, chunk)] = ready.reshape(chunk, capacity, 2 * LANES)

        def give(i, carry):
            to = j * chunk + i

            @pl.when(to != me)
            def _():
                push(send_two, recv_two, sems.at[4], sems.at[5], to)

            return carry

        lax.fori_loop(0, chunk, give, 0)
    keep_own(send_two, recv_two, sems.at[5])

    arrived(recv_slot, sems.at[3])
    total_slots = n * capacity
    got = recv_slot[...].reshape(n, LANES).astype(BF16)
    source_of = iota((total_slots, n), 0) // capacity == iota((total_slots, n), 1)
    got = jnp.dot(one_hot(source_of).astype(BF16), got, preferred_element_type=F32)
    wanted = iota((total_slots, LANES), 0) % capacity == iota((total_slots, LANES), 1)
    got = jnp.sum(jnp.where(wanted, got, 0.0), 1, keepdims=True).astype(jnp.int32)
    select = one_hot(got == iota((total_slots, LANES), 1)).T[:rows_out].astype(BF16)
    arrived(recv_two, sems.at[5])
    landed = recv_two[...].reshape(total_slots, 2 * LANES)
    image = jnp.dot(select, landed, preferred_element_type=F32) * scale
    out_ref[:, 0, :] = image[:, :LANES]
    out_ref[:, 1, :] = image[:, LANES:]
    departed(send_one, sems.at[0])
    departed(send_slot, sems.at[2])
    departed(send_two, sems.at[4])


def per_device(
    n,
    pa,
    raw_pulses,
    chirp_taps,
    steer_angle,
    interp_weights,
    tile_phase,
    tap_offset,
    image_slot,
    tile_owner,
):
    pulses, _, length = raw_pulses.shape
    _, count_a, count_beams = steer_angle.shape
    tiles = tile_owner.shape[2]
    count_tiles = count_beams * tiles
    capacity = 2 * count_tiles // n
    chunk = PLANE if n % PLANE == 0 else n
    blocks = length // LANES
    width = pulses * 2 * blocks // n
    reach = chirp_taps.shape[1] // LANES
    spread_factor = float(pa * count_tiles // IMG_ROWS) ** (-0.5)
    operands = (
        raw_pulses,
        chirp_taps,
        steer_angle.reshape(count_a, count_beams),
        tile_owner.transpose(0, 2, 1).reshape(tiles, count_beams),
        image_slot.transpose(0, 2, 1).reshape(tiles, count_beams),
        interp_weights.transpose(0, 1, 3, 2).reshape(4, tiles, count_beams),
        tile_phase.transpose(0, 2, 1).reshape(tiles, count_beams),
        tap_offset.transpose(0, 2, 1).reshape(tiles, count_beams),
    )
    image_part = pl.pallas_call(
        functools.partial(body, n, IMG_ROWS, spread_factor),
        out_shape=pltpu.VMEM((IMG_ROWS, 2, LANES), F32),
        in_specs=[pl.BlockSpec(memory_space=pltpu.HBM)] * len(operands),
        out_specs=pl.BlockSpec(memory_space=pltpu.VMEM),
        scratch_shapes=[pltpu.VMEM(x.shape, x.dtype) for x in operands]
        + [
            pltpu.VMEM((pulses, 2 * blocks + 2 * reach, LANES), F32),
            pltpu.VMEM((n, width, LANES), BF16),
            pltpu.VMEM((n, width, LANES), BF16),
            pltpu.VMEM((n, 1, LANES), F32),
            pltpu.VMEM((n, 1, LANES), F32),
            pltpu.VMEM((n, capacity, 2 * LANES), BF16),
            pltpu.VMEM((n, capacity, 2 * LANES), BF16),
            pltpu.VMEM((count_tiles, 2 * n * width), BF16),
            pltpu.VMEM((n // chunk, 2 * chunk * capacity, n * width), BF16),
            pltpu.VMEM((n // chunk, WEIGHTS, chunk * capacity, LANES), F32),
            pltpu.VMEM((n // chunk, chunk * capacity, LANES), jnp.int32),
            pltpu.VMEM((n * capacity, count_tiles), BF16),
            pltpu.SemaphoreType.DMA((6,)),
            pltpu.SemaphoreType.DMA((len(operands),)),
        ],
        compiler_params=pltpu.CompilerParams(
            collective_id=0, has_side_effects=True, vmem_limit_bytes=62 << 20
        ),
    )(*operands)
    if pa > 1:
        image_part = lax.psum_scatter(image_part, "pa", scatter_dimension=0, tiled=True)
    return image_part[None]


def solution(mesh):
    placed = (
        P(("pa", "row"), None, None),
        P(),
        P("pa", None, None),
        P(None, "pa", None, "row"),
        P("pa", None, "row"),
        P("pa", None, "row"),
        P("pa", None, "row"),
        P("pa", None, "row"),
    )
    return jax.shard_map(
        functools.partial(per_device, mesh.shape["row"], mesh.shape["pa"]),
        mesh=mesh,
        in_specs=placed,
        out_specs=P("row", "pa", None, None),
        check_vma=False,
    )
```

```python
import functools

import jax
import jax.numpy as jnp
from jax import lax
from jax.experimental import pallas as pl
from jax.experimental.pallas import tpu as pltpu
from jax.sharding import PartitionSpec as P

LANES = 128
IMG_ROWS = 64
F32 = jnp.float32
BF16 = jnp.bfloat16
NT = (((1,), (1,)), ((), ()))
TN = (((0,), (0,)), ((), ()))
WEIGHTS = 4
LOW = (0, 2, 3, 1)
HIGH = (2, 3, 0, 1)
OUTER = (0, 1, 2, 3)
SCHEDULE = ((2, 2, 0, 0), (0, 0, 1, 1), (4, 4, 4, 4), (1, 1, 3, 2), (3, 3, 2, 3), (7, 7, 7, 7))


def iota(shape, dim):
    return lax.broadcasted_iota(jnp.int32, shape, dim)


def one_hot(cond):
    return jnp.where(cond, 1.0, 0.0)


def mirrored(me, n, i):
    if n & (n - 1):
        return lax.rem(me + i, n)
    return jnp.bitwise_xor(me, n - i)


def body(
    n,
    rows_out,
    scale,
    x_hbm,
    taps_hbm,
    angle_hbm,
    owner_hbm,
    slot_hbm,
    weight_hbm,
    phase_hbm,
    offset_hbm,
    out_ref,
    x_ref,
    taps_ref,
    angle_ref,
    owner_ref,
    slot_ref,
    weight_ref,
    phase_ref,
    offset_ref,
    xs,
    meta,
    send_one,
    recv_one,
    send_slot,
    recv_slot,
    send_two,
    recv_two,
    steer,
    packed,
    coeff,
    turn,
    turning,
    sems,
    load_sems,
):
    me = lax.axis_index("row")
    pulses, _, length = x_ref.shape
    blocks = length // LANES
    reach = taps_ref.shape[1] // LANES
    group = 2 * blocks // n
    width = pulses * group
    tiles = group // 2
    count_a, count_beams = angle_ref.shape
    count_tiles = tiles * count_beams
    capacity = send_two.shape[1]
    chunk = n // 4
    rows = chunk * capacity
    half = 2 * chunk
    side = lax.div(me, half)
    outer = jnp.logical_or(me < chunk, me >= n - chunk)
    mirror = jnp.where(side == 0, me + n - chunk, me - n + chunk)

    given = (x_hbm, taps_hbm, angle_hbm, owner_hbm, slot_hbm, weight_hbm, phase_hbm, offset_hbm)
    held = (x_ref, taps_ref, angle_ref, owner_ref, slot_ref, weight_ref, phase_ref, offset_ref)
    held_copies = [
        pltpu.make_async_copy(source, target, load_sems.at[index])
        for index, (source, target) in enumerate(zip(given, held))
    ]
    barrier = pltpu.get_barrier_semaphore()

    def greet(i, carry):
        pl.semaphore_signal(barrier, inc=1, device_id={"row": lax.rem(me + i, n)})
        return carry

    lax.fori_loop(1, n, greet, 0)
    for copy in held_copies:
        copy.start()

    for index in (3, 4, 5, 6, 7):
        held_copies[index].wait()
    weights = weight_ref[...].astype(F32)
    fields = [owner_ref[...].astype(F32), slot_ref[...].astype(F32)]
    fields += [weights[k] for k in range(WEIGHTS)]
    fields += [offset_ref[...].astype(F32), phase_ref[...].astype(F32)]
    meta[0] = jnp.concatenate(
        [jnp.concatenate([f[t : t + 1, :] for t in range(tiles)], 1) for f in fields], 0
    )

    held_copies[0].wait()
    for p in range(pulses):
        for b in range(blocks):
            piece = x_ref[p, :, b * LANES : (b + 1) * LANES]
            xs[p, 2 * b : 2 * b + 2, :] = piece.astype(F32)
        xs[p, 2 * blocks :, :] = jnp.zeros((2 * reach, LANES), F32)
    keep = iota((LANES, LANES), 1) >= iota((LANES, LANES), 0)
    zero = jnp.zeros((LANES, LANES), F32)
    held_copies[1].wait()
    halves = []
    for c in range(2):
        rolled = []
        for j in range(reach):
            row = taps_ref[c : c + 1, j * LANES : (j + 1) * LANES].astype(F32)
            row = jnp.broadcast_to(row, (LANES, LANES))
            rolled.append(pltpu.roll(row, 0, 1, stride=1, stride_axis=0))
        rolled = [zero] + rolled + [zero]
        halves.append(
            jnp.concatenate(
                [jnp.where(keep, rolled[j + 1], rolled[j]).astype(BF16) for j in range(reach + 1)], 1
            )
        )
    band = jnp.concatenate(halves, 0)
    outs = []
    parity = iota((2 * blocks, LANES), 0) % 2 == 0
    for p in range(pulses):
        window = jnp.concatenate(
            [xs[p, 2 * j : 2 * j + 2 * blocks, :].astype(BF16) for j in range(reach + 1)], 1
        )
        product = lax.dot_general(window, band, NT, preferred_element_type=F32)
        first, second = product[:, :LANES], product[:, LANES:]
        crossed = jnp.where(
            parity, pltpu.roll(second, 2 * blocks - 1, 0), -pltpu.roll(second, 1, 0)
        )
        outs.append((first + crossed).reshape(n, group, LANES))
    send_one[...] = jnp.concatenate(outs, 1).astype(BF16)

    pl.semaphore_wait(barrier, n - 1)

    def push(source, target, send_sem, recv_sem, to):
        pltpu.make_async_remote_copy(
            src_ref=source,
            dst_ref=target,
            send_sem=send_sem,
            recv_sem=recv_sem,
            device_id={"row": to},
        ).start()

    def keep_own(source, target, recv_sem):
        pltpu.make_async_copy(source, target, recv_sem).start()

    def exchange(source_of, target, send_sem, recv_sem):
        def first(i, carry):
            @pl.when(i != me)
            def _():
                push(source_of(i), target, send_sem, recv_sem, i)

            return carry

        def rest(i, carry):
            to = mirrored(me, n, i)

            @pl.when(to >= 2)
            def _():
                push(source_of(to), target, send_sem, recv_sem, to)

            return carry

        lax.fori_loop(0, 2, first, 0)
        lax.fori_loop(1, n, rest, 0)
        keep_own(source_of(me), target, recv_sem)

    def arrived(target, recv_sem):
        pltpu.make_async_copy(target, target, recv_sem).wait()

    departed = arrived

    @pl.when(outer)
    def _():
        push(meta.at[0], meta.at[1], sems.at[6], sems.at[7], mirror)

    plane_here, place_here = lax.div(me, chunk), lax.rem(me, chunk)

    def spread(plane, copy):
        shifted_plane = jnp.where(copy == 1, 3 - plane, plane)

        def one(i, carry):
            place = mirrored(place_here, chunk, i)
            to = plane * chunk + place
            source = send_one.at[shifted_plane * chunk + place]
            target = recv_one.at[copy, me]
            recv_sem = sems.at[1 + 7 * copy]

            @pl.when(to != me)
            def _():
                push(source, target, sems.at[0], recv_sem, to)

            @pl.when(to == me)
            def _():
                keep_own(source, target, recv_sem)

            return carry

        lax.fori_loop(1, chunk + 1, one, 0)

    for turn_of in SCHEDULE:
        code = jnp.where(
            plane_here < 2,
            jnp.where(plane_here == 0, turn_of[0], turn_of[1]),
            jnp.where(plane_here == 2, turn_of[2], turn_of[3]),
        )
        spread(lax.rem(code, 4), lax.div(code, 4))

    before = one_hot(iota((count_tiles, count_tiles), 0) < iota((count_tiles, count_tiles), 1))
    before = before.astype(BF16)

    def ranked_tiles(known):
        owner = known[0:1].astype(jnp.int32)
        member = one_hot(owner == iota((n, count_tiles), 0))
        ahead = jnp.dot(member.astype(BF16), before, preferred_element_type=F32)
        rank = jnp.sum(ahead * member, 0, keepdims=True).astype(jnp.int32)
        return owner, member, rank

    known = meta[0]
    owner, member, rank = ranked_tiles(known)
    ranked = jnp.where(rank == iota((LANES, count_tiles), 0), known[1:2], 0.0)
    slots = lax.dot_general(
        member.astype(BF16), ranked.astype(BF16), NT, preferred_element_type=F32
    )
    send_slot[...] = slots.reshape(n, 1, LANES)
    exchange(lambda to: send_slot.at[to], recv_slot.at[me], sems.at[2], sems.at[3])

    held_copies[2].wait()
    span = n * width
    pulse_of = iota((count_a, span), 1) // group == iota((count_a, span), 0)
    expand = one_hot(pulse_of).astype(BF16)
    angles = angle_ref[...]
    cosine = lax.dot_general(
        jnp.cos(angles).astype(BF16), expand, TN, preferred_element_type=F32
    )
    sine = lax.dot_general(
        jnp.sin(angles).astype(BF16), expand, TN, preferred_element_type=F32
    )
    column = iota((count_beams, span), 1) % group
    even = column % 2 == 0
    turning[0] = jnp.where(even, cosine, -sine)
    turning[1] = jnp.where(even, sine, cosine)
    norm = count_a ** (-0.5)

    def prepare(known, owner, rank, begin, first, count):
        depth = count * rows
        near = lax.rem(owner + n - side * half, n) - begin
        place = near * capacity + rank
        pack = one_hot(place == iota((depth, count_tiles), 0)).astype(BF16)
        table = jnp.concatenate([known, jnp.zeros_like(known)], 0).astype(BF16)
        columns = lax.dot_general(pack, table, NT, preferred_element_type=F32)
        lane = iota((depth, LANES), 1)
        offset = jnp.broadcast_to(
            columns[:, 2 + WEIGHTS : 3 + WEIGHTS], (depth, LANES)
        ).astype(jnp.int32)
        turn[first : first + count] = (2 - offset).reshape(count, rows, LANES)
        for k in range(WEIGHTS):
            reached = lane + offset + (k - 1)
            inside = (reached >= 0) & (reached < LANES)
            level = jnp.where(inside, columns[:, 2 + k : 3 + k], 0.0)
            coeff[k, first : first + count] = level.reshape(count, rows, LANES)
        phases = known[3 + WEIGHTS : 4 + WEIGHTS]
        turns = [norm * jnp.cos(phases), norm * jnp.sin(phases)]
        turns = [
            f[:, t * count_beams : (t + 1) * count_beams] for f in turns for t in range(tiles)
        ]
        turns.append(jnp.zeros((LANES - 2 * tiles, count_beams), F32))
        turns = jnp.concatenate(turns, 0).T
        for t in range(tiles):
            here = column // 2 == t
            c = turns[:, t : t + 1]
            s = turns[:, tiles + t : tiles + t + 1]
            base = t * count_beams
            steer[base : base + count_beams, :span] = jnp.where(
                here, c * turning[0] - s * turning[1], 0.0
            ).astype(BF16)
            steer[base : base + count_beams, span:] = jnp.where(
                here, s * turning[0] + c * turning[1], 0.0
            ).astype(BF16)
        for j in range(count):
            part = jnp.dot(
                pack[j * rows : (j + 1) * rows], steer[...], preferred_element_type=F32
            ).astype(BF16)
            packed[first + j, :rows, :] = part[:, :span]
            packed[first + j, rows:, :] = part[:, span:]

    def form(turned, entry, begin, block):
        formed = jnp.dot(packed[entry], turned, preferred_element_type=F32)
        by = turn[entry]
        one, two, four = by % 2 == 1, by // 2 % 2 == 1, by >= 4
        taps = [coeff[k, entry] for k in range(WEIGHTS)]
        shifted = []
        for c in range(2):
            x = formed[c * rows : (c + 1) * rows]
            x = jnp.where(one, x, pltpu.roll(x, LANES - 1, 1))
            x = jnp.where(two, pltpu.roll(x, 2, 1), x)
            x = jnp.where(four, pltpu.roll(x, 4, 1), x)
            total = taps[0] * x
            for k in range(1, WEIGHTS):
                total = total + taps[k] * pltpu.roll(x, LANES - k, 1)
            shifted.append(total)
        ready = jnp.concatenate(shifted, 1).astype(BF16)
        at = entry * chunk
        send_two[pl.ds(at, chunk)] = ready.reshape(chunk, capacity, 2 * LANES)

        def give(i, carry):
            to = lax.rem(begin + i + side * half, n)

            @pl.when(to != me)
            def _():
                push(send_two.at[at + i], recv_two.at[block], sems.at[4], sems.at[5], to)

            @pl.when(to == me)
            def _():
                keep_own(send_two.at[at + i], recv_two.at[block], sems.at[5])

            return carry

        lax.fori_loop(0, chunk, give, 0)

    prepare(known, owner, rank, 0, 0, 2)

    @pl.when(outer)
    def _():
        arrived(meta.at[1], sems.at[7])

    other = jnp.where(outer, 1, 0)
    known = meta[other]
    owner, member, rank = ranked_tiles(known)
    begin = jnp.where(outer, 0, half)
    prepare(known, owner, rank, begin, 2, 2)
    arrived(recv_one.at[0], sems.at[1])
    for step in range(4):
        if step == OUTER.index(2):

            @pl.when(outer)
            def _():
                arrived(recv_one.at[1], sems.at[8])

        entry = jnp.where(outer, OUTER[step], jnp.where(side == 0, LOW[step], HIGH[step]))
        late = lax.div(entry, 2)
        moved = late * other
        turned = recv_one[moved].reshape(span, LANES)
        form(
            turned,
            entry,
            lax.rem(entry, 2) * chunk + late * begin,
            jnp.where(moved == 1, mirror, me),
        )

    arrived(recv_slot, sems.at[3])
    total_slots = n * capacity
    got = recv_slot[...].reshape(n, LANES).astype(BF16)
    source_of = iota((total_slots, n), 0) // capacity == iota((total_slots, n), 1)
    got = jnp.dot(one_hot(source_of).astype(BF16), got, preferred_element_type=F32)
    wanted = iota((total_slots, LANES), 0) % capacity == iota((total_slots, LANES), 1)
    got = jnp.sum(jnp.where(wanted, got, 0.0), 1, keepdims=True).astype(jnp.int32)
    select = one_hot(got == iota((total_slots, LANES), 1)).T[:rows_out].astype(BF16)
    arrived(recv_two, sems.at[5])
    landed = recv_two[...].reshape(total_slots, 2 * LANES)
    image = jnp.dot(select, landed, preferred_element_type=F32) * scale
    out_ref[:, 0, :] = image[:, :LANES]
    out_ref[:, 1, :] = image[:, LANES:]
    departed(send_slot.at[pl.ds(0, n - 1)], sems.at[2])
    departed(recv_one.at[0, pl.ds(0, n - 1)], sems.at[0])

    @pl.when(outer)
    def _():
        departed(meta.at[0], sems.at[6])
        departed(recv_one.at[0, pl.ds(0, 2 * chunk - 1)], sems.at[0])
        departed(send_two.at[pl.ds(0, n - 2)], sems.at[4])

    @pl.when(jnp.logical_not(outer))
    def _():
        departed(recv_one.at[0, pl.ds(0, 2 * chunk)], sems.at[0])
        departed(send_two.at[pl.ds(0, n - 1)], sems.at[4])


def per_device(
    n,
    pa,
    raw_pulses,
    chirp_taps,
    steer_angle,
    interp_weights,
    tile_phase,
    tap_offset,
    image_slot,
    tile_owner,
):
    pulses, _, length = raw_pulses.shape
    _, count_a, count_beams = steer_angle.shape
    tiles = tile_owner.shape[2]
    count_tiles = count_beams * tiles
    capacity = 2 * count_tiles // n
    groups, chunk = 4, n // 4
    rows = chunk * capacity
    blocks = length // LANES
    width = pulses * 2 * blocks // n
    reach = chirp_taps.shape[1] // LANES
    spread_factor = float(pa * count_tiles // IMG_ROWS) ** (-0.5)
    operands = (
        raw_pulses,
        chirp_taps,
        steer_angle.reshape(count_a, count_beams),
        tile_owner.transpose(0, 2, 1).reshape(tiles, count_beams),
        image_slot.transpose(0, 2, 1).reshape(tiles, count_beams),
        interp_weights.transpose(0, 1, 3, 2).reshape(4, tiles, count_beams),
        tile_phase.transpose(0, 2, 1).reshape(tiles, count_beams),
        tap_offset.transpose(0, 2, 1).reshape(tiles, count_beams),
    )
    image_part = pl.pallas_call(
        functools.partial(body, n, IMG_ROWS, spread_factor),
        out_shape=pltpu.VMEM((IMG_ROWS, 2, LANES), F32),
        in_specs=[pl.BlockSpec(memory_space=pltpu.HBM)] * len(operands),
        out_specs=pl.BlockSpec(memory_space=pltpu.VMEM),
        scratch_shapes=[pltpu.VMEM(x.shape, x.dtype) for x in operands]
        + [
            pltpu.VMEM((pulses, 2 * blocks + 2 * reach, LANES), F32),
            pltpu.VMEM((2, 8, count_tiles), F32),
            pltpu.VMEM((n, width, LANES), BF16),
            pltpu.VMEM((2, n, width, LANES), BF16),
            pltpu.VMEM((n, 1, LANES), F32),
            pltpu.VMEM((n, 1, LANES), F32),
            pltpu.VMEM((n, capacity, 2 * LANES), BF16),
            pltpu.VMEM((n, capacity, 2 * LANES), BF16),
            pltpu.VMEM((count_tiles, 2 * n * width), BF16),
            pltpu.VMEM((groups, 2 * rows, n * width), BF16),
            pltpu.VMEM((WEIGHTS, groups, rows, LANES), F32),
            pltpu.VMEM((groups, rows, LANES), jnp.int32),
            pltpu.VMEM((2, count_beams, n * width), F32),
            pltpu.SemaphoreType.DMA((9,)),
            pltpu.SemaphoreType.DMA((len(operands),)),
        ],
        compiler_params=pltpu.CompilerParams(
            collective_id=0, has_side_effects=True, vmem_limit_bytes=62 << 20
        ),
    )(*operands)
    if pa > 1:
        image_part = lax.psum_scatter(image_part, "pa", scatter_dimension=0, tiled=True)
    return image_part[None]


def solution(mesh):
    placed = (
        P(("pa", "row"), None, None),
        P(),
        P("pa", None, None),
        P(None, "pa", None, "row"),
        P("pa", None, "row"),
        P("pa", None, "row"),
        P("pa", None, "row"),
        P("pa", None, "row"),
    )
    return jax.shard_map(
        functools.partial(per_device, mesh.shape["row"], mesh.shape["pa"]),
        mesh=mesh,
        in_specs=placed,
        out_specs=P("row", "pa", None, None),
        check_vma=False,
    )
```

```python
import functools

import jax
import jax.numpy as jnp
from jax import lax
from jax.experimental import pallas as pl
from jax.experimental.pallas import tpu as pltpu
from jax.sharding import PartitionSpec as P

LANES = 128
IMG_ROWS = 64
F32 = jnp.float32
BF16 = jnp.bfloat16
NT = (((1,), (1,)), ((), ()))
TN = (((0,), (0,)), ((), ()))
WEIGHTS = 4
LOW = (0, 2, 3, 1)
HIGH = (2, 3, 0, 1)
OUTER = (0, 1, 2, 3)
SCHEDULE = ((2, 2, 0, 0), (0, 0, 1, 1), (4, 4, 4, 4), (1, 1, 3, 2), (3, 3, 2, 3), (7, 7, 7, 7))


def iota(shape, dim):
    return lax.broadcasted_iota(jnp.int32, shape, dim)


def one_hot(cond):
    return jnp.where(cond, 1.0, 0.0)


def mirrored(me, n, i):
    if n & (n - 1):
        return lax.rem(me + i, n)
    return jnp.bitwise_xor(me, n - i)


def body(
    n,
    rows_out,
    scale,
    x_hbm,
    taps_hbm,
    angle_hbm,
    owner_hbm,
    slot_hbm,
    weight_hbm,
    phase_hbm,
    offset_hbm,
    out_ref,
    x_ref,
    taps_ref,
    angle_ref,
    owner_ref,
    slot_ref,
    weight_ref,
    phase_ref,
    offset_ref,
    xs,
    meta,
    send_one,
    recv_one,
    send_slot,
    recv_slot,
    send_two,
    recv_two,
    steer,
    packed,
    coeff,
    turn,
    turning,
    sems,
    load_sems,
    entered,
):
    me = lax.axis_index("row")
    pulses, _, length = x_ref.shape
    blocks = length // LANES
    reach = taps_ref.shape[1] // LANES
    group = 2 * blocks // n
    width = pulses * group
    tiles = group // 2
    count_a, count_beams = angle_ref.shape
    count_tiles = tiles * count_beams
    capacity = send_two.shape[1]
    chunk = n // 4
    rows = chunk * capacity
    half = 2 * chunk
    side = lax.div(me, half)
    outer = jnp.logical_or(me < chunk, me >= n - chunk)
    mirror = jnp.where(side == 0, me + n - chunk, me - n + chunk)

    given = (x_hbm, taps_hbm, angle_hbm, owner_hbm, slot_hbm, weight_hbm, phase_hbm, offset_hbm)
    held = (x_ref, taps_ref, angle_ref, owner_ref, slot_ref, weight_ref, phase_ref, offset_ref)
    held_copies = [
        pltpu.make_async_copy(source, target, load_sems.at[index])
        for index, (source, target) in enumerate(zip(given, held))
    ]
    barrier = pltpu.get_barrier_semaphore()

    def greet(i, carry):
        to = (1 - side) * half + lax.rem(me + i, half)
        pl.semaphore_signal(barrier, inc=1, device_id={"row": to})
        return carry

    lax.fori_loop(0, half, greet, 0)
    for copy in held_copies:
        copy.start()

    for index in (3, 4, 5, 6, 7):
        held_copies[index].wait()
    weights = weight_ref[...].astype(F32)
    fields = [owner_ref[...].astype(F32), slot_ref[...].astype(F32)]
    fields += [weights[k] for k in range(WEIGHTS)]
    fields += [offset_ref[...].astype(F32), phase_ref[...].astype(F32)]
    meta[0] = jnp.concatenate(
        [jnp.concatenate([f[t : t + 1, :] for t in range(tiles)], 1) for f in fields], 0
    )

    held_copies[0].wait()
    for p in range(pulses):
        for b in range(blocks):
            piece = x_ref[p, :, b * LANES : (b + 1) * LANES]
            xs[p, 2 * b : 2 * b + 2, :] = piece.astype(F32)
        xs[p, 2 * blocks :, :] = jnp.zeros((2 * reach, LANES), F32)
    keep = iota((LANES, LANES), 1) >= iota((LANES, LANES), 0)
    zero = jnp.zeros((LANES, LANES), F32)
    held_copies[1].wait()
    halves = []
    for c in range(2):
        rolled = []
        for j in range(reach):
            row = taps_ref[c : c + 1, j * LANES : (j + 1) * LANES].astype(F32)
            row = jnp.broadcast_to(row, (LANES, LANES))
            rolled.append(pltpu.roll(row, 0, 1, stride=1, stride_axis=0))
        rolled = [zero] + rolled + [zero]
        halves.append(
            jnp.concatenate(
                [jnp.where(keep, rolled[j + 1], rolled[j]).astype(BF16) for j in range(reach + 1)], 1
            )
        )
    band = jnp.concatenate(halves, 0)
    outs = []
    parity = iota((2 * blocks, LANES), 0) % 2 == 0
    for p in range(pulses):
        window = jnp.concatenate(
            [xs[p, 2 * j : 2 * j + 2 * blocks, :].astype(BF16) for j in range(reach + 1)], 1
        )
        product = lax.dot_general(window, band, NT, preferred_element_type=F32)
        first, second = product[:, :LANES], product[:, LANES:]
        crossed = jnp.where(
            parity, pltpu.roll(second, 2 * blocks - 1, 0), -pltpu.roll(second, 1, 0)
        )
        outs.append((first + crossed).reshape(n, group, LANES))
    send_one[...] = jnp.concatenate(outs, 1).astype(BF16)

    pl.semaphore_wait(barrier, half)
    plane_here, place_here = lax.div(me, chunk), lax.rem(me, chunk)

    @pl.when(jnp.logical_not(outer))
    def _():
        for plane in range(2):
            to = ((1 - side) * 2 + plane) * chunk + place_here
            pl.semaphore_signal(entered, inc=1, device_id={"row": to})


    def push(source, target, send_sem, recv_sem, to):
        pltpu.make_async_remote_copy(
            src_ref=source,
            dst_ref=target,
            send_sem=send_sem,
            recv_sem=recv_sem,
            device_id={"row": to},
        ).start()

    def keep_own(source, target, recv_sem):
        pltpu.make_async_copy(source, target, recv_sem).start()

    def exchange(source_of, target, send_sem, recv_sem):
        def first(i, carry):
            @pl.when(i != me)
            def _():
                push(source_of(i), target, send_sem, recv_sem, i)

            return carry

        def rest(i, carry):
            to = mirrored(me, n, i)

            @pl.when(to >= 2)
            def _():
                push(source_of(to), target, send_sem, recv_sem, to)

            return carry

        lax.fori_loop(0, 2, first, 0)
        lax.fori_loop(1, n, rest, 0)
        keep_own(source_of(me), target, recv_sem)

    def arrived(target, recv_sem):
        pltpu.make_async_copy(target, target, recv_sem).wait()

    departed = arrived

    @pl.when(outer)
    def _():
        push(meta.at[0], meta.at[1], sems.at[6], sems.at[7], mirror)

    def spread(plane, copy):
        shifted_plane = jnp.where(copy == 1, 3 - plane, plane)

        def one(i, carry):
            place = mirrored(place_here, chunk, i)
            to = plane * chunk + place
            source = send_one.at[shifted_plane * chunk + place]
            target = recv_one.at[copy, me]
            recv_sem = sems.at[1 + 7 * copy]

            @pl.when(to != me)
            def _():
                push(source, target, sems.at[0], recv_sem, to)

            @pl.when(to == me)
            def _():
                keep_own(source, target, recv_sem)

            return carry

        lax.fori_loop(1, chunk + 1, one, 0)

    for order, turn_of in enumerate(SCHEDULE):
        if order in (0, 3):

            @pl.when(side == (0 if order == 0 else 1))
            def _():
                pl.semaphore_wait(entered, 1)

        code = jnp.where(
            plane_here < 2,
            jnp.where(plane_here == 0, turn_of[0], turn_of[1]),
            jnp.where(plane_here == 2, turn_of[2], turn_of[3]),
        )
        spread(lax.rem(code, 4), lax.div(code, 4))

    before = one_hot(iota((count_tiles, count_tiles), 0) < iota((count_tiles, count_tiles), 1))
    before = before.astype(BF16)

    def ranked_tiles(known):
        owner = known[0:1].astype(jnp.int32)
        member = one_hot(owner == iota((n, count_tiles), 0))
        ahead = jnp.dot(member.astype(BF16), before, preferred_element_type=F32)
        rank = jnp.sum(ahead * member, 0, keepdims=True).astype(jnp.int32)
        return owner, member, rank

    known = meta[0]
    owner, member, rank = ranked_tiles(known)
    ranked = jnp.where(rank == iota((LANES, count_tiles), 0), known[1:2], 0.0)
    slots = lax.dot_general(
        member.astype(BF16), ranked.astype(BF16), NT, preferred_element_type=F32
    )
    send_slot[...] = slots.reshape(n, 1, LANES)
    exchange(lambda to: send_slot.at[to], recv_slot.at[me], sems.at[2], sems.at[3])

    held_copies[2].wait()
    span = n * width
    pulse_of = iota((count_a, span), 1) // group == iota((count_a, span), 0)
    expand = one_hot(pulse_of).astype(BF16)
    angles = angle_ref[...]
    cosine = lax.dot_general(
        jnp.cos(angles).astype(BF16), expand, TN, preferred_element_type=F32
    )
    sine = lax.dot_general(
        jnp.sin(angles).astype(BF16), expand, TN, preferred_element_type=F32
    )
    column = iota((count_beams, span), 1) % group
    even = column % 2 == 0
    turning[0] = jnp.where(even, cosine, -sine)
    turning[1] = jnp.where(even, sine, cosine)
    norm = count_a ** (-0.5)

    def prepare(known, owner, rank, begin, first, count):
        depth = count * rows
        near = lax.rem(owner + n - side * half, n) - begin
        place = near * capacity + rank
        pack = one_hot(place == iota((depth, count_tiles), 0)).astype(BF16)
        table = jnp.concatenate([known, jnp.zeros_like(known)], 0).astype(BF16)
        columns = lax.dot_general(pack, table, NT, preferred_element_type=F32)
        lane = iota((depth, LANES), 1)
        offset = jnp.broadcast_to(
            columns[:, 2 + WEIGHTS : 3 + WEIGHTS], (depth, LANES)
        ).astype(jnp.int32)
        turn[first : first + count] = (2 - offset).reshape(count, rows, LANES)
        for k in range(WEIGHTS):
            reached = lane + offset + (k - 1)
            inside = (reached >= 0) & (reached < LANES)
            level = jnp.where(inside, columns[:, 2 + k : 3 + k], 0.0)
            coeff[k, first : first + count] = level.reshape(count, rows, LANES)
        phases = known[3 + WEIGHTS : 4 + WEIGHTS]
        turns = [norm * jnp.cos(phases), norm * jnp.sin(phases)]
        turns = [
            f[:, t * count_beams : (t + 1) * count_beams] for f in turns for t in range(tiles)
        ]
        turns.append(jnp.zeros((LANES - 2 * tiles, count_beams), F32))
        turns = jnp.concatenate(turns, 0).T
        for t in range(tiles):
            here = column // 2 == t
            c = turns[:, t : t + 1]
            s = turns[:, tiles + t : tiles + t + 1]
            base = t * count_beams
            steer[base : base + count_beams, :span] = jnp.where(
                here, c * turning[0] - s * turning[1], 0.0
            ).astype(BF16)
            steer[base : base + count_beams, span:] = jnp.where(
                here, s * turning[0] + c * turning[1], 0.0
            ).astype(BF16)
        for j in range(count):
            part = jnp.dot(
                pack[j * rows : (j + 1) * rows], steer[...], preferred_element_type=F32
            ).astype(BF16)
            packed[first + j, :rows, :] = part[:, :span]
            packed[first + j, rows:, :] = part[:, span:]

    def form(turned, entry, begin, block):
        formed = jnp.dot(packed[entry], turned, preferred_element_type=F32)
        by = turn[entry]
        one, two, four = by % 2 == 1, by // 2 % 2 == 1, by >= 4
        taps = [coeff[k, entry] for k in range(WEIGHTS)]
        shifted = []
        for c in range(2):
            x = formed[c * rows : (c + 1) * rows]
            x = jnp.where(one, x, pltpu.roll(x, LANES - 1, 1))
            x = jnp.where(two, pltpu.roll(x, 2, 1), x)
            x = jnp.where(four, pltpu.roll(x, 4, 1), x)
            total = taps[0] * x
            for k in range(1, WEIGHTS):
                total = total + taps[k] * pltpu.roll(x, LANES - k, 1)
            shifted.append(total)
        ready = jnp.concatenate(shifted, 1).astype(BF16)
        at = entry * chunk
        send_two[pl.ds(at, chunk)] = ready.reshape(chunk, capacity, 2 * LANES)

        def give(i, carry):
            to = lax.rem(begin + i + side * half, n)

            @pl.when(to != me)
            def _():
                push(send_two.at[at + i], recv_two.at[block], sems.at[4], sems.at[5], to)

            @pl.when(to == me)
            def _():
                keep_own(send_two.at[at + i], recv_two.at[block], sems.at[5])

            return carry

        lax.fori_loop(0, chunk, give, 0)

    prepare(known, owner, rank, 0, 0, 2)

    @pl.when(outer)
    def _():
        arrived(meta.at[1], sems.at[7])

    other = jnp.where(outer, 1, 0)
    known = meta[other]
    owner, member, rank = ranked_tiles(known)
    begin = jnp.where(outer, 0, half)
    prepare(known, owner, rank, begin, 2, 2)
    arrived(recv_one.at[0], sems.at[1])
    for step in range(4):
        if step == OUTER.index(2):

            @pl.when(outer)
            def _():
                arrived(recv_one.at[1], sems.at[8])

        entry = jnp.where(outer, OUTER[step], jnp.where(side == 0, LOW[step], HIGH[step]))
        late = lax.div(entry, 2)
        moved = late * other
        turned = recv_one[moved].reshape(span, LANES)
        form(
            turned,
            entry,
            lax.rem(entry, 2) * chunk + late * begin,
            jnp.where(moved == 1, mirror, me),
        )

    arrived(recv_slot, sems.at[3])
    total_slots = n * capacity
    got = recv_slot[...].reshape(n, LANES).astype(BF16)
    source_of = iota((total_slots, n), 0) // capacity == iota((total_slots, n), 1)
    got = jnp.dot(one_hot(source_of).astype(BF16), got, preferred_element_type=F32)
    wanted = iota((total_slots, LANES), 0) % capacity == iota((total_slots, LANES), 1)
    got = jnp.sum(jnp.where(wanted, got, 0.0), 1, keepdims=True).astype(jnp.int32)
    select = one_hot(got == iota((total_slots, LANES), 1)).T[:rows_out].astype(BF16)
    arrived(recv_two, sems.at[5])
    landed = recv_two[...].reshape(total_slots, 2 * LANES)
    image = jnp.dot(select, landed, preferred_element_type=F32) * scale
    out_ref[:, 0, :] = image[:, :LANES]
    out_ref[:, 1, :] = image[:, LANES:]
    departed(send_slot.at[pl.ds(0, n - 1)], sems.at[2])
    departed(recv_one.at[0, pl.ds(0, n - 1)], sems.at[0])

    @pl.when(outer)
    def _():
        departed(meta.at[0], sems.at[6])
        departed(recv_one.at[0, pl.ds(0, 2 * chunk - 1)], sems.at[0])
        departed(send_two.at[pl.ds(0, n - 2)], sems.at[4])

    @pl.when(jnp.logical_not(outer))
    def _():
        departed(recv_one.at[0, pl.ds(0, 2 * chunk)], sems.at[0])
        departed(send_two.at[pl.ds(0, n - 1)], sems.at[4])


def per_device(
    n,
    pa,
    raw_pulses,
    chirp_taps,
    steer_angle,
    interp_weights,
    tile_phase,
    tap_offset,
    image_slot,
    tile_owner,
):
    pulses, _, length = raw_pulses.shape
    _, count_a, count_beams = steer_angle.shape
    tiles = tile_owner.shape[2]
    count_tiles = count_beams * tiles
    capacity = 2 * count_tiles // n
    groups, chunk = 4, n // 4
    rows = chunk * capacity
    blocks = length // LANES
    width = pulses * 2 * blocks // n
    reach = chirp_taps.shape[1] // LANES
    spread_factor = float(pa * count_tiles // IMG_ROWS) ** (-0.5)
    operands = (
        raw_pulses,
        chirp_taps,
        steer_angle.reshape(count_a, count_beams),
        tile_owner.transpose(0, 2, 1).reshape(tiles, count_beams),
        image_slot.transpose(0, 2, 1).reshape(tiles, count_beams),
        interp_weights.transpose(0, 1, 3, 2).reshape(4, tiles, count_beams),
        tile_phase.transpose(0, 2, 1).reshape(tiles, count_beams),
        tap_offset.transpose(0, 2, 1).reshape(tiles, count_beams),
    )
    image_part = pl.pallas_call(
        functools.partial(body, n, IMG_ROWS, spread_factor),
        out_shape=pltpu.VMEM((IMG_ROWS, 2, LANES), F32),
        in_specs=[pl.BlockSpec(memory_space=pltpu.HBM)] * len(operands),
        out_specs=pl.BlockSpec(memory_space=pltpu.VMEM),
        scratch_shapes=[pltpu.VMEM(x.shape, x.dtype) for x in operands]
        + [
            pltpu.VMEM((pulses, 2 * blocks + 2 * reach, LANES), F32),
            pltpu.VMEM((2, 8, count_tiles), F32),
            pltpu.VMEM((n, width, LANES), BF16),
            pltpu.VMEM((2, n, width, LANES), BF16),
            pltpu.VMEM((n, 1, LANES), F32),
            pltpu.VMEM((n, 1, LANES), F32),
            pltpu.VMEM((n, capacity, 2 * LANES), BF16),
            pltpu.VMEM((n, capacity, 2 * LANES), BF16),
            pltpu.VMEM((count_tiles, 2 * n * width), BF16),
            pltpu.VMEM((groups, 2 * rows, n * width), BF16),
            pltpu.VMEM((WEIGHTS, groups, rows, LANES), F32),
            pltpu.VMEM((groups, rows, LANES), jnp.int32),
            pltpu.VMEM((2, count_beams, n * width), F32),
            pltpu.SemaphoreType.DMA((9,)),
            pltpu.SemaphoreType.DMA((len(operands),)),
            pltpu.SemaphoreType.REGULAR,
        ],
        compiler_params=pltpu.CompilerParams(
            collective_id=0, has_side_effects=True, vmem_limit_bytes=62 << 20
        ),
    )(*operands)
    if pa > 1:
        image_part = lax.psum_scatter(image_part, "pa", scatter_dimension=0, tiled=True)
    return image_part[None]


def solution(mesh):
    placed = (
        P(("pa", "row"), None, None),
        P(),
        P("pa", None, None),
        P(None, "pa", None, "row"),
        P("pa", None, "row"),
        P("pa", None, "row"),
        P("pa", None, "row"),
        P("pa", None, "row"),
    )
    return jax.shard_map(
        functools.partial(per_device, mesh.shape["row"], mesh.shape["pa"]),
        mesh=mesh,
        in_specs=placed,
        out_specs=P("row", "pa", None, None),
        check_vma=False,
    )
```

```python
import functools

import jax
import jax.numpy as jnp
from jax import lax
from jax.experimental import pallas as pl
from jax.experimental.pallas import tpu as pltpu
from jax.sharding import PartitionSpec as P

LANES = 128
IMG_ROWS = 64
F32 = jnp.float32
BF16 = jnp.bfloat16
NT = (((1,), (1,)), ((), ()))
TN = (((0,), (0,)), ((), ()))
WEIGHTS = 4
LOW = (0, 2, 3, 1)
HIGH = (2, 3, 0, 1)
OUTER = (0, 1, 2, 3)
SCHEDULE = ((2, 2, 0, 0), (0, 0, 1, 1), (4, 3, 4, 4), (1, 7, 3, 2), (3, 4, 2, 3), (7, 1, 7, 7))


def iota(shape, dim):
    return lax.broadcasted_iota(jnp.int32, shape, dim)


def one_hot(cond):
    return jnp.where(cond, 1.0, 0.0)


def mirrored(me, n, i):
    if n & (n - 1):
        return lax.rem(me + i, n)
    return jnp.bitwise_xor(me, n - i)


def body(
    n,
    rows_out,
    scale,
    x_hbm,
    taps_hbm,
    angle_hbm,
    owner_hbm,
    slot_hbm,
    weight_hbm,
    phase_hbm,
    offset_hbm,
    out_ref,
    x_ref,
    taps_ref,
    angle_ref,
    owner_ref,
    slot_ref,
    weight_ref,
    phase_ref,
    offset_ref,
    xs,
    meta,
    send_one,
    recv_one,
    send_slot,
    recv_slot,
    send_two,
    recv_two,
    steer,
    packed,
    coeff,
    turn,
    turning,
    sems,
    load_sems,
    entered,
):
    me = lax.axis_index("row")
    pulses, blocks = x_ref.shape[0], x_ref.shape[1] // 2
    reach = taps_ref.shape[1] // LANES
    group = 2 * blocks // n
    width = pulses * group
    tiles = group // 2
    count_a, count_beams = angle_ref.shape
    count_tiles = tiles * count_beams
    capacity = send_two.shape[1]
    chunk = n // 4
    rows = chunk * capacity
    half = 2 * chunk
    side = lax.div(me, half)
    outer = jnp.logical_or(me < chunk, me >= n - chunk)
    mirror = jnp.where(side == 0, me + n - chunk, me - n + chunk)

    given = (x_hbm, taps_hbm, angle_hbm, owner_hbm, slot_hbm, weight_hbm, phase_hbm, offset_hbm)
    held = (x_ref, taps_ref, angle_ref, owner_ref, slot_ref, weight_ref, phase_ref, offset_ref)
    held_copies = [
        pltpu.make_async_copy(source, target, load_sems.at[index])
        for index, (source, target) in enumerate(zip(given, held))
    ]
    for copy in held_copies[:2]:
        copy.start()
    barrier = pltpu.get_barrier_semaphore()

    def greet(i, carry):
        to = (1 - side) * half + lax.rem(me + i, half)
        pl.semaphore_signal(barrier, inc=1, device_id={"row": to})
        return carry

    lax.fori_loop(0, half, greet, 0)
    for copy in held_copies[2:]:
        copy.start()

    keep = iota((LANES, LANES), 1) >= iota((LANES, LANES), 0)
    zero = jnp.zeros((LANES, LANES), F32)
    held_copies[1].wait()
    halves = []
    for c in range(2):
        rolled = []
        for j in range(reach):
            row = taps_ref[c : c + 1, j * LANES : (j + 1) * LANES].astype(F32)
            row = jnp.broadcast_to(row, (LANES, LANES))
            rolled.append(pltpu.roll(row, 0, 1, stride=1, stride_axis=0))
        rolled = [zero] + rolled + [zero]
        halves.append(
            jnp.concatenate(
                [jnp.where(keep, rolled[j + 1], rolled[j]).astype(BF16) for j in range(reach + 1)], 1
            )
        )
    band = jnp.concatenate(halves, 0)

    for index in (3, 4, 5, 6, 7):
        held_copies[index].wait()
    weights = weight_ref[...].astype(F32)
    fields = [owner_ref[...].astype(F32), slot_ref[...].astype(F32)]
    fields += [weights[k] for k in range(WEIGHTS)]
    fields += [offset_ref[...].astype(F32), phase_ref[...].astype(F32)]
    meta[0] = jnp.concatenate(
        [jnp.concatenate([f[t : t + 1, :] for t in range(tiles)], 1) for f in fields], 0
    )

    held_copies[0].wait()
    for p in range(pulses):
        xs[p, : 2 * blocks, :] = x_ref[p].astype(F32)
        xs[p, 2 * blocks :, :] = jnp.zeros((2 * reach, LANES), F32)
    outs = []
    parity = iota((2 * blocks, LANES), 0) % 2 == 0
    for p in range(pulses):
        window = jnp.concatenate(
            [xs[p, 2 * j : 2 * j + 2 * blocks, :].astype(BF16) for j in range(reach + 1)], 1
        )
        product = lax.dot_general(window, band, NT, preferred_element_type=F32)
        first, second = product[:, :LANES], product[:, LANES:]
        crossed = jnp.where(
            parity, pltpu.roll(second, 2 * blocks - 1, 0), -pltpu.roll(second, 1, 0)
        )
        outs.append((first + crossed).reshape(n, group, LANES))
    send_one[...] = jnp.concatenate(outs, 1).astype(BF16)

    pl.semaphore_wait(barrier, half)
    plane_here, place_here = lax.div(me, chunk), lax.rem(me, chunk)

    @pl.when(jnp.logical_not(outer))
    def _():
        for plane in range(2):
            to = ((1 - side) * 2 + plane) * chunk + place_here
            pl.semaphore_signal(entered, inc=1, device_id={"row": to})


    def push(source, target, send_sem, recv_sem, to):
        pltpu.make_async_remote_copy(
            src_ref=source,
            dst_ref=target,
            send_sem=send_sem,
            recv_sem=recv_sem,
            device_id={"row": to},
        ).start()

    def keep_own(source, target, recv_sem):
        pltpu.make_async_copy(source, target, recv_sem).start()

    def exchange(source_of, target, send_sem, recv_sem):
        def first(i, carry):
            @pl.when(i != me)
            def _():
                push(source_of(i), target, send_sem, recv_sem, i)

            return carry

        def rest(i, carry):
            to = mirrored(me, n, i)

            @pl.when(to >= 2)
            def _():
                push(source_of(to), target, send_sem, recv_sem, to)

            return carry

        lax.fori_loop(0, 2, first, 0)
        lax.fori_loop(1, n, rest, 0)
        keep_own(source_of(me), target, recv_sem)

    def arrived(target, recv_sem):
        pltpu.make_async_copy(target, target, recv_sem).wait()

    departed = arrived

    @pl.when(outer)
    def _():
        push(meta.at[0], meta.at[1], sems.at[6], sems.at[7], mirror)

    def spread(plane, copy):
        shifted_plane = jnp.where(copy == 1, 3 - plane, plane)

        def one(i, carry):
            place = mirrored(place_here, chunk, i)
            to = plane * chunk + place
            source = send_one.at[shifted_plane * chunk + place]
            target = recv_one.at[copy, me]
            recv_sem = sems.at[1 + 7 * copy]

            @pl.when(to != me)
            def _():
                push(source, target, sems.at[0], recv_sem, to)

            @pl.when(to == me)
            def _():
                keep_own(source, target, recv_sem)

            return carry

        lax.fori_loop(1, chunk + 1, one, 0)

    for order, turn_of in enumerate(SCHEDULE):
        if order in (0, 3):

            @pl.when(side == (0 if order == 0 else 1))
            def _():
                pl.semaphore_wait(entered, 1)

        code = jnp.where(
            plane_here < 2,
            jnp.where(plane_here == 0, turn_of[0], turn_of[1]),
            jnp.where(plane_here == 2, turn_of[2], turn_of[3]),
        )
        spread(lax.rem(code, 4), lax.div(code, 4))

    before = one_hot(iota((count_tiles, count_tiles), 0) < iota((count_tiles, count_tiles), 1))
    before = before.astype(BF16)

    def ranked_tiles(known):
        owner = known[0:1].astype(jnp.int32)
        member = one_hot(owner == iota((n, count_tiles), 0))
        ahead = jnp.dot(member.astype(BF16), before, preferred_element_type=F32)
        rank = jnp.sum(ahead * member, 0, keepdims=True).astype(jnp.int32)
        return owner, member, rank

    known = meta[0]
    owner, member, rank = ranked_tiles(known)
    ranked = jnp.where(rank == iota((LANES, count_tiles), 0), known[1:2], 0.0)
    slots = lax.dot_general(
        member.astype(BF16), ranked.astype(BF16), NT, preferred_element_type=F32
    )
    send_slot[...] = slots.reshape(n, 1, LANES)
    exchange(lambda to: send_slot.at[to], recv_slot.at[me], sems.at[2], sems.at[3])

    held_copies[2].wait()
    span = n * width
    pulse_of = iota((count_a, span), 1) // group == iota((count_a, span), 0)
    expand = one_hot(pulse_of).astype(BF16)
    angles = angle_ref[...]
    cosine = lax.dot_general(
        jnp.cos(angles).astype(BF16), expand, TN, preferred_element_type=F32
    )
    sine = lax.dot_general(
        jnp.sin(angles).astype(BF16), expand, TN, preferred_element_type=F32
    )
    column = iota((count_beams, span), 1) % group
    even = column % 2 == 0
    turning[0] = jnp.where(even, cosine, -sine)
    turning[1] = jnp.where(even, sine, cosine)
    norm = count_a ** (-0.5)

    def prepare(known, owner, rank, begin, first, count):
        depth = count * rows
        near = lax.rem(owner + n - side * half, n) - begin
        place = near * capacity + rank
        pack = one_hot(place == iota((depth, count_tiles), 0)).astype(BF16)
        table = jnp.concatenate([known, jnp.zeros_like(known)], 0).astype(BF16)
        columns = lax.dot_general(pack, table, NT, preferred_element_type=F32)
        lane = iota((depth, LANES), 1)
        offset = jnp.broadcast_to(
            columns[:, 2 + WEIGHTS : 3 + WEIGHTS], (depth, LANES)
        ).astype(jnp.int32)
        turn[first : first + count] = (2 - offset).reshape(count, rows, LANES)
        for k in range(WEIGHTS):
            reached = lane + offset + (k - 1)
            inside = (reached >= 0) & (reached < LANES)
            level = jnp.where(inside, columns[:, 2 + k : 3 + k], 0.0)
            coeff[k, first : first + count] = level.reshape(count, rows, LANES)
        phases = known[3 + WEIGHTS : 4 + WEIGHTS]
        turns = [norm * jnp.cos(phases), norm * jnp.sin(phases)]
        turns = [
            f[:, t * count_beams : (t + 1) * count_beams] for f in turns for t in range(tiles)
        ]
        turns.append(jnp.zeros((LANES - 2 * tiles, count_beams), F32))
        turns = jnp.concatenate(turns, 0).T
        for t in range(tiles):
            here = column // 2 == t
            c = turns[:, t : t + 1]
            s = turns[:, tiles + t : tiles + t + 1]
            base = t * count_beams
            steer[base : base + count_beams, :span] = jnp.where(
                here, c * turning[0] - s * turning[1], 0.0
            ).astype(BF16)
            steer[base : base + count_beams, span:] = jnp.where(
                here, s * turning[0] + c * turning[1], 0.0
            ).astype(BF16)
        for j in range(count):
            part = jnp.dot(
                pack[j * rows : (j + 1) * rows], steer[...], preferred_element_type=F32
            ).astype(BF16)
            packed[first + j, :rows, :] = part[:, :span]
            packed[first + j, rows:, :] = part[:, span:]

    def form(turned, entry, begin, block):
        formed = jnp.dot(packed[entry], turned, preferred_element_type=F32)
        by = turn[entry]
        one, two, four = (by & 1) == 1, (by & 2) == 2, by >= 4
        taps = [coeff[k, entry] for k in range(WEIGHTS)]
        shifted = []
        for c in range(2):
            x = formed[c * rows : (c + 1) * rows]
            x = jnp.where(one, x, pltpu.roll(x, LANES - 1, 1))
            x = jnp.where(two, pltpu.roll(x, 2, 1), x)
            x = jnp.where(four, pltpu.roll(x, 4, 1), x)
            total = taps[0] * x
            for k in range(1, WEIGHTS):
                total = total + taps[k] * pltpu.roll(x, LANES - k, 1)
            shifted.append(total)
        ready = jnp.concatenate(shifted, 1).astype(BF16)
        at = entry * chunk
        send_two[pl.ds(at, chunk)] = ready.reshape(chunk, capacity, 2 * LANES)

        def give(step, carry):
            pair = lax.div(step, 2)
            swap = jnp.where(pair == 1, 2, jnp.where(pair == 2, -2, 0)) if chunk == 8 else 0
            i = step + swap
            to = lax.rem(begin + i + side * half, n)

            @pl.when(to != me)
            def _():
                push(send_two.at[at + i], recv_two.at[block], sems.at[4], sems.at[5], to)

            @pl.when(to == me)
            def _():
                keep_own(send_two.at[at + i], recv_two.at[block], sems.at[5])

            return carry

        lax.fori_loop(0, chunk, give, 0)

    prepare(known, owner, rank, 0, 0, 2)

    @pl.when(outer)
    def _():
        arrived(meta.at[1], sems.at[7])

    other = jnp.where(outer, 1, 0)
    known = meta[other]
    owner, member, rank = ranked_tiles(known)
    begin = jnp.where(outer, 0, half)
    prepare(known, owner, rank, begin, 2, 2)
    arrived(recv_one.at[0], sems.at[1])
    for step in range(4):
        if step == OUTER.index(2):

            @pl.when(outer)
            def _():
                arrived(recv_one.at[1], sems.at[8])

        entry = jnp.where(outer, OUTER[step], jnp.where(side == 0, LOW[step], HIGH[step]))
        late = lax.div(entry, 2)
        moved = late * other
        turned = recv_one[moved].reshape(span, LANES)
        form(
            turned,
            entry,
            lax.rem(entry, 2) * chunk + late * begin,
            jnp.where(moved == 1, mirror, me),
        )

    arrived(recv_slot, sems.at[3])
    total_slots = n * capacity
    got = recv_slot[...].reshape(n, LANES).astype(BF16)
    source_of = iota((total_slots, n), 0) // capacity == iota((total_slots, n), 1)
    got = jnp.dot(one_hot(source_of).astype(BF16), got, preferred_element_type=F32)
    wanted = iota((total_slots, LANES), 0) % capacity == iota((total_slots, LANES), 1)
    got = jnp.sum(jnp.where(wanted, got, 0.0), 1, keepdims=True).astype(jnp.int32)
    select = one_hot(got == iota((total_slots, LANES), 1)).T[:rows_out].astype(BF16)
    arrived(recv_two, sems.at[5])
    landed = recv_two[...].reshape(total_slots, 2 * LANES)
    image = jnp.dot(select, landed, preferred_element_type=F32) * scale
    out_ref[:, 0, :] = image[:, :LANES]
    out_ref[:, 1, :] = image[:, LANES:]
    departed(send_slot.at[pl.ds(0, n - 1)], sems.at[2])
    departed(recv_one.at[0, pl.ds(0, n - 1)], sems.at[0])

    @pl.when(outer)
    def _():
        departed(meta.at[0], sems.at[6])
        departed(recv_one.at[0, pl.ds(0, 2 * chunk - 1)], sems.at[0])
        departed(send_two.at[pl.ds(0, n - 2)], sems.at[4])

    @pl.when(jnp.logical_not(outer))
    def _():
        departed(recv_one.at[0, pl.ds(0, 2 * chunk)], sems.at[0])
        departed(send_two.at[pl.ds(0, n - 1)], sems.at[4])


def per_device(
    n,
    pa,
    raw_pulses,
    chirp_taps,
    steer_angle,
    interp_weights,
    tile_phase,
    tap_offset,
    image_slot,
    tile_owner,
):
    pulses, _, length = raw_pulses.shape
    _, count_a, count_beams = steer_angle.shape
    tiles = tile_owner.shape[2]
    count_tiles = count_beams * tiles
    capacity = 2 * count_tiles // n
    groups, chunk = 4, n // 4
    rows = chunk * capacity
    blocks = length // LANES
    width = pulses * 2 * blocks // n
    reach = chirp_taps.shape[1] // LANES
    spread_factor = float(pa * count_tiles // IMG_ROWS) ** (-0.5)
    lines = raw_pulses.reshape(pulses, 2, blocks, LANES).transpose(0, 2, 1, 3)
    operands = (
        lines.reshape(pulses, 2 * blocks, LANES),
        chirp_taps,
        steer_angle.reshape(count_a, count_beams),
        tile_owner.transpose(0, 2, 1).reshape(tiles, count_beams),
        image_slot.transpose(0, 2, 1).reshape(tiles, count_beams),
        interp_weights.transpose(0, 1, 3, 2).reshape(4, tiles, count_beams),
        tile_phase.transpose(0, 2, 1).reshape(tiles, count_beams),
        tap_offset.transpose(0, 2, 1).reshape(tiles, count_beams),
    )
    image_part = pl.pallas_call(
        functools.partial(body, n, IMG_ROWS, spread_factor),
        out_shape=pltpu.VMEM((IMG_ROWS, 2, LANES), F32),
        in_specs=[pl.BlockSpec(memory_space=pltpu.HBM)] * len(operands),
        out_specs=pl.BlockSpec(memory_space=pltpu.VMEM),
        scratch_shapes=[pltpu.VMEM(x.shape, x.dtype) for x in operands]
        + [
            pltpu.VMEM((pulses, 2 * blocks + 2 * reach, LANES), F32),
            pltpu.VMEM((2, 8, count_tiles), F32),
            pltpu.VMEM((n, width, LANES), BF16),
            pltpu.VMEM((2, n, width, LANES), BF16),
            pltpu.VMEM((n, 1, LANES), F32),
            pltpu.VMEM((n, 1, LANES), F32),
            pltpu.VMEM((n, capacity, 2 * LANES), BF16),
            pltpu.VMEM((n, capacity, 2 * LANES), BF16),
            pltpu.VMEM((count_tiles, 2 * n * width), BF16),
            pltpu.VMEM((groups, 2 * rows, n * width), BF16),
            pltpu.VMEM((WEIGHTS, groups, rows, LANES), F32),
            pltpu.VMEM((groups, rows, LANES), jnp.int32),
            pltpu.VMEM((2, count_beams, n * width), F32),
            pltpu.SemaphoreType.DMA((9,)),
            pltpu.SemaphoreType.DMA((len(operands),)),
            pltpu.SemaphoreType.REGULAR,
        ],
        compiler_params=pltpu.CompilerParams(
            collective_id=0, has_side_effects=True, vmem_limit_bytes=62 << 20
        ),
    )(*operands)
    if pa > 1:
        image_part = lax.psum_scatter(image_part, "pa", scatter_dimension=0, tiled=True)
    return image_part[None]


def solution(mesh):
    placed = (
        P(("pa", "row"), None, None),
        P(),
        P("pa", None, None),
        P(None, "pa", None, "row"),
        P("pa", None, "row"),
        P("pa", None, "row"),
        P("pa", None, "row"),
        P("pa", None, "row"),
    )
    return jax.shard_map(
        functools.partial(per_device, mesh.shape["row"], mesh.shape["pa"]),
        mesh=mesh,
        in_specs=placed,
        out_specs=P("row", "pa", None, None),
        check_vma=False,
    )
```

```python
import functools

import jax
import jax.numpy as jnp
from jax import lax
from jax.experimental import pallas as pl
from jax.experimental.pallas import tpu as pltpu
from jax.sharding import PartitionSpec as P

LANES = 128
IMG_ROWS = 64
F32 = jnp.float32
BF16 = jnp.bfloat16
NT = (((1,), (1,)), ((), ()))
TN = (((0,), (0,)), ((), ()))
WEIGHTS = 4
LOW = (0, 2, 3, 1)
HIGH = (2, 3, 0, 1)
OUTER = (0, 1, 2, 3)
SCHEDULE = ((2, 2, 0, 0), (0, 0, 1, 1), (4, 3, 4, 4), (1, 7, 3, 2), (3, 4, 2, 3), (7, 1, 7, 7))


def iota(shape, dim):
    return lax.broadcasted_iota(jnp.int32, shape, dim)


def one_hot(cond):
    return jnp.where(cond, 1.0, 0.0)


def mirrored(me, n, i):
    if n & (n - 1):
        return lax.rem(me + i, n)
    return jnp.bitwise_xor(me, n - i)


def body(
    n,
    rows_out,
    scale,
    x_hbm,
    taps_hbm,
    angle_hbm,
    owner_hbm,
    slot_hbm,
    weight_hbm,
    phase_hbm,
    offset_hbm,
    out_ref,
    x_ref,
    taps_ref,
    angle_ref,
    owner_ref,
    slot_ref,
    weight_ref,
    phase_ref,
    offset_ref,
    xs,
    meta,
    send_one,
    recv_one,
    send_slot,
    recv_slot,
    send_two,
    recv_two,
    steer,
    packed,
    coeff,
    turn,
    turning,
    sems,
    load_sems,
    entered,
):
    me = lax.axis_index("row")
    pulses, blocks = x_ref.shape[0], x_ref.shape[1] // 2
    reach = taps_ref.shape[1] // LANES
    group = 2 * blocks // n
    width = pulses * group
    tiles = group // 2
    count_a, count_beams = angle_ref.shape
    count_tiles = tiles * count_beams
    capacity = send_two.shape[1]
    chunk = n // 4
    rows = chunk * capacity
    half = 2 * chunk
    side = lax.div(me, half)
    outer = jnp.logical_or(me < chunk, me >= n - chunk)
    mirror = jnp.where(side == 0, me + n - chunk, me - n + chunk)

    given = (x_hbm, taps_hbm, angle_hbm, owner_hbm, slot_hbm, weight_hbm, phase_hbm, offset_hbm)
    held = (x_ref, taps_ref, angle_ref, owner_ref, slot_ref, weight_ref, phase_ref, offset_ref)
    held_copies = [
        pltpu.make_async_copy(source, target, load_sems.at[index])
        for index, (source, target) in enumerate(zip(given, held))
    ]
    for copy in held_copies[:2]:
        copy.start()
    barrier = pltpu.get_barrier_semaphore()

    def greet(i, carry):
        to = (1 - side) * half + i
        pl.semaphore_signal(barrier, inc=1, device_id={"row": to})
        return carry

    lax.fori_loop(0, half, greet, 0)
    for copy in held_copies[2:]:
        copy.start()

    keep = iota((LANES, LANES), 1) >= iota((LANES, LANES), 0)
    zero = jnp.zeros((LANES, LANES), F32)
    held_copies[1].wait()
    halves = []
    for c in range(2):
        rolled = []
        for j in range(reach):
            row = taps_ref[c : c + 1, j * LANES : (j + 1) * LANES].astype(F32)
            row = jnp.broadcast_to(row, (LANES, LANES))
            rolled.append(pltpu.roll(row, 0, 1, stride=1, stride_axis=0))
        rolled = [zero] + rolled + [zero]
        halves.append(
            jnp.concatenate(
                [jnp.where(keep, rolled[j + 1], rolled[j]).astype(BF16) for j in range(reach + 1)], 1
            )
        )
    band = jnp.concatenate(halves, 0)

    for index in (3, 4, 5, 6, 7):
        held_copies[index].wait()
    weights = weight_ref[...].astype(F32)
    fields = [owner_ref[...].astype(F32), slot_ref[...].astype(F32)]
    fields += [weights[k] for k in range(WEIGHTS)]
    fields += [offset_ref[...].astype(F32), phase_ref[...].astype(F32)]
    meta[0] = jnp.concatenate(
        [jnp.concatenate([f[t : t + 1, :] for t in range(tiles)], 1) for f in fields], 0
    )

    held_copies[0].wait()
    for p in range(pulses):
        xs[p, : 2 * blocks, :] = x_ref[p].astype(F32)
        xs[p, 2 * blocks :, :] = jnp.zeros((2 * reach, LANES), F32)
    outs = []
    parity = iota((2 * blocks, LANES), 0) % 2 == 0
    for p in range(pulses):
        window = jnp.concatenate(
            [xs[p, 2 * j : 2 * j + 2 * blocks, :].astype(BF16) for j in range(reach + 1)], 1
        )
        product = lax.dot_general(window, band, NT, preferred_element_type=F32)
        first, second = product[:, :LANES], product[:, LANES:]
        crossed = jnp.where(
            parity, pltpu.roll(second, 2 * blocks - 1, 0), -pltpu.roll(second, 1, 0)
        )
        outs.append((first + crossed).reshape(n, group, LANES))
    send_one[...] = jnp.concatenate(outs, 1).astype(BF16)

    pl.semaphore_wait(barrier, half)
    plane_here, place_here = lax.div(me, chunk), lax.rem(me, chunk)

    @pl.when(jnp.logical_not(outer))
    def _():
        for plane in range(2):
            to = ((1 - side) * 2 + plane) * chunk + place_here
            pl.semaphore_signal(entered, inc=1, device_id={"row": to})


    def push(source, target, send_sem, recv_sem, to):
        pltpu.make_async_remote_copy(
            src_ref=source,
            dst_ref=target,
            send_sem=send_sem,
            recv_sem=recv_sem,
            device_id={"row": to},
        ).start()

    def keep_own(source, target, recv_sem):
        pltpu.make_async_copy(source, target, recv_sem).start()

    def exchange(source_of, target, send_sem, recv_sem):
        def first(i, carry):
            @pl.when(i != me)
            def _():
                push(source_of(i), target, send_sem, recv_sem, i)

            return carry

        def rest(i, carry):
            to = mirrored(me, n, i)

            @pl.when(to >= 2)
            def _():
                push(source_of(to), target, send_sem, recv_sem, to)

            return carry

        lax.fori_loop(0, 2, first, 0)
        lax.fori_loop(1, n, rest, 0)
        keep_own(source_of(me), target, recv_sem)

    def arrived(target, recv_sem):
        pltpu.make_async_copy(target, target, recv_sem).wait()

    departed = arrived

    @pl.when(outer)
    def _():
        push(meta.at[0], meta.at[1], sems.at[6], sems.at[7], mirror)

    def spread(plane, copy):
        shifted_plane = jnp.where(copy == 1, 3 - plane, plane)

        def one(i, carry):
            place = mirrored(place_here, chunk, i)
            to = plane * chunk + place
            source = send_one.at[shifted_plane * chunk + place]
            target = recv_one.at[copy, me]
            recv_sem = sems.at[1 + 7 * copy]

            @pl.when(to != me)
            def _():
                push(source, target, sems.at[0], recv_sem, to)

            @pl.when(to == me)
            def _():
                keep_own(source, target, recv_sem)

            return carry

        lax.fori_loop(1, chunk + 1, one, 0)

    for order, turn_of in enumerate(SCHEDULE):
        if order in (0, 3):

            @pl.when(side == (0 if order == 0 else 1))
            def _():
                pl.semaphore_wait(entered, 1)

        code = jnp.where(
            plane_here < 2,
            jnp.where(plane_here == 0, turn_of[0], turn_of[1]),
            jnp.where(plane_here == 2, turn_of[2], turn_of[3]),
        )
        spread(lax.rem(code, 4), lax.div(code, 4))

    before = one_hot(iota((count_tiles, count_tiles), 0) < iota((count_tiles, count_tiles), 1))
    before = before.astype(BF16)

    def ranked_tiles(known):
        owner = known[0:1].astype(jnp.int32)
        member = one_hot(owner == iota((n, count_tiles), 0))
        ahead = jnp.dot(member.astype(BF16), before, preferred_element_type=F32)
        rank = jnp.sum(ahead * member, 0, keepdims=True).astype(jnp.int32)
        return owner, member, rank

    known = meta[0]
    owner, member, rank = ranked_tiles(known)
    ranked = jnp.where(rank == iota((LANES, count_tiles), 0), known[1:2], 0.0)
    slots = lax.dot_general(
        member.astype(BF16), ranked.astype(BF16), NT, preferred_element_type=F32
    )
    send_slot[...] = slots.reshape(n, 1, LANES)

    held_copies[2].wait()
    span = n * width
    pulse_of = iota((count_a, span), 1) // group == iota((count_a, span), 0)
    expand = one_hot(pulse_of).astype(BF16)
    angles = angle_ref[...]
    cosine = lax.dot_general(
        jnp.cos(angles).astype(BF16), expand, TN, preferred_element_type=F32
    )
    sine = lax.dot_general(
        jnp.sin(angles).astype(BF16), expand, TN, preferred_element_type=F32
    )
    column = iota((count_beams, span), 1) % group
    even = column % 2 == 0
    turning[0] = jnp.where(even, cosine, -sine)
    turning[1] = jnp.where(even, sine, cosine)
    norm = count_a ** (-0.5)

    def prepare(known, owner, rank, begin, first, count):
        depth = count * rows
        near = lax.rem(owner + n - side * half, n) - begin
        place = near * capacity + rank
        pack = one_hot(place == iota((depth, count_tiles), 0)).astype(BF16)
        table = jnp.concatenate([known, jnp.zeros_like(known)], 0).astype(BF16)
        columns = lax.dot_general(pack, table, NT, preferred_element_type=F32)
        lane = iota((depth, LANES), 1)
        offset = jnp.broadcast_to(
            columns[:, 2 + WEIGHTS : 3 + WEIGHTS], (depth, LANES)
        ).astype(jnp.int32)
        turn[first : first + count] = (2 - offset).reshape(count, rows, LANES)
        for k in range(WEIGHTS):
            reached = lane + offset + (k - 1)
            inside = (reached >= 0) & (reached < LANES)
            level = jnp.where(inside, columns[:, 2 + k : 3 + k], 0.0)
            coeff[k, first : first + count] = level.reshape(count, rows, LANES)
        phases = known[3 + WEIGHTS : 4 + WEIGHTS]
        turns = [norm * jnp.cos(phases), norm * jnp.sin(phases)]
        turns = [
            f[:, t * count_beams : (t + 1) * count_beams] for f in turns for t in range(tiles)
        ]
        turns.append(jnp.zeros((LANES - 2 * tiles, count_beams), F32))
        turns = jnp.concatenate(turns, 0).T
        for t in range(tiles):
            here = column // 2 == t
            c = turns[:, t : t + 1]
            s = turns[:, tiles + t : tiles + t + 1]
            base = t * count_beams
            steer[base : base + count_beams, :span] = jnp.where(
                here, c * turning[0] - s * turning[1], 0.0
            ).astype(BF16)
            steer[base : base + count_beams, span:] = jnp.where(
                here, s * turning[0] + c * turning[1], 0.0
            ).astype(BF16)
        for j in range(count):
            part = jnp.dot(
                pack[j * rows : (j + 1) * rows], steer[...], preferred_element_type=F32
            ).astype(BF16)
            packed[first + j, :rows, :] = part[:, :span]
            packed[first + j, rows:, :] = part[:, span:]

    def form(turned, entry, begin, block):
        formed = jnp.dot(packed[entry], turned, preferred_element_type=F32)
        by = turn[entry]
        one, two, four = (by & 1) == 1, (by & 2) == 2, by >= 4
        taps = [coeff[k, entry] for k in range(WEIGHTS)]
        shifted = []
        for c in range(2):
            x = formed[c * rows : (c + 1) * rows]
            x = jnp.where(one, x, pltpu.roll(x, LANES - 1, 1))
            x = jnp.where(two, pltpu.roll(x, 2, 1), x)
            x = jnp.where(four, pltpu.roll(x, 4, 1), x)
            total = taps[0] * x
            for k in range(1, WEIGHTS):
                total = total + taps[k] * pltpu.roll(x, LANES - k, 1)
            shifted.append(total)
        ready = jnp.concatenate(shifted, 1).astype(BF16)
        at = entry * chunk
        send_two[pl.ds(at, chunk)] = ready.reshape(chunk, capacity, 2 * LANES)

        def give(step, carry):
            pair = lax.div(step, 2)
            swap = jnp.where(pair == 1, 2, jnp.where(pair == 2, -2, 0)) if chunk == 8 else 0
            i = step + swap
            to = lax.rem(begin + i + side * half, n)

            @pl.when(to != me)
            def _():
                push(send_two.at[at + i], recv_two.at[block], sems.at[4], sems.at[5], to)

            @pl.when(to == me)
            def _():
                keep_own(send_two.at[at + i], recv_two.at[block], sems.at[5])

            return carry

        lax.fori_loop(0, chunk, give, 0)

    prepare(known, owner, rank, 0, 0, 2)

    @pl.when(outer)
    def _():
        arrived(meta.at[1], sems.at[7])

    other = jnp.where(outer, 1, 0)
    known = meta[other]
    owner, member, rank = ranked_tiles(known)
    begin = jnp.where(outer, 0, half)
    prepare(known, owner, rank, begin, 2, 2)
    exchange(lambda to: send_slot.at[to], recv_slot.at[me], sems.at[2], sems.at[3])
    arrived(recv_one.at[0], sems.at[1])
    for step in range(4):
        if step == OUTER.index(2):

            @pl.when(outer)
            def _():
                arrived(recv_one.at[1], sems.at[8])

        entry = jnp.where(outer, OUTER[step], jnp.where(side == 0, LOW[step], HIGH[step]))
        late = lax.div(entry, 2)
        moved = late * other
        turned = recv_one[moved].reshape(span, LANES)
        form(
            turned,
            entry,
            lax.rem(entry, 2) * chunk + late * begin,
            jnp.where(moved == 1, mirror, me),
        )

    arrived(recv_slot, sems.at[3])
    total_slots = n * capacity
    got = recv_slot[...].reshape(n, LANES).astype(BF16)
    source_of = iota((total_slots, n), 0) // capacity == iota((total_slots, n), 1)
    got = jnp.dot(one_hot(source_of).astype(BF16), got, preferred_element_type=F32)
    wanted = iota((total_slots, LANES), 0) % capacity == iota((total_slots, LANES), 1)
    got = jnp.sum(jnp.where(wanted, got, 0.0), 1, keepdims=True).astype(jnp.int32)
    select = one_hot(got == iota((total_slots, LANES), 1)).T[:rows_out].astype(BF16)
    arrived(recv_two, sems.at[5])
    landed = recv_two[...].reshape(total_slots, 2 * LANES)
    image = jnp.dot(select, landed, preferred_element_type=F32) * scale
    out_ref[:, 0, :] = image[:, :LANES]
    out_ref[:, 1, :] = image[:, LANES:]
    departed(send_slot.at[pl.ds(0, n - 1)], sems.at[2])
    departed(recv_one.at[0, pl.ds(0, n - 1)], sems.at[0])

    @pl.when(outer)
    def _():
        departed(meta.at[0], sems.at[6])
        departed(recv_one.at[0, pl.ds(0, 2 * chunk - 1)], sems.at[0])
        departed(send_two.at[pl.ds(0, n - 2)], sems.at[4])

    @pl.when(jnp.logical_not(outer))
    def _():
        departed(recv_one.at[0, pl.ds(0, 2 * chunk)], sems.at[0])
        departed(send_two.at[pl.ds(0, n - 1)], sems.at[4])


def per_device(
    n,
    pa,
    raw_pulses,
    chirp_taps,
    steer_angle,
    interp_weights,
    tile_phase,
    tap_offset,
    image_slot,
    tile_owner,
):
    pulses, _, length = raw_pulses.shape
    _, count_a, count_beams = steer_angle.shape
    tiles = tile_owner.shape[2]
    count_tiles = count_beams * tiles
    capacity = 2 * count_tiles // n
    groups, chunk = 4, n // 4
    rows = chunk * capacity
    blocks = length // LANES
    width = pulses * 2 * blocks // n
    reach = chirp_taps.shape[1] // LANES
    spread_factor = float(pa * count_tiles // IMG_ROWS) ** (-0.5)
    lines = raw_pulses.reshape(pulses, 2, blocks, LANES).transpose(0, 2, 1, 3)
    operands = (
        lines.reshape(pulses, 2 * blocks, LANES),
        chirp_taps,
        steer_angle.reshape(count_a, count_beams),
        tile_owner.transpose(0, 2, 1).reshape(tiles, count_beams),
        image_slot.transpose(0, 2, 1).reshape(tiles, count_beams),
        interp_weights.transpose(0, 1, 3, 2).reshape(4, tiles, count_beams),
        tile_phase.transpose(0, 2, 1).reshape(tiles, count_beams),
        tap_offset.transpose(0, 2, 1).reshape(tiles, count_beams),
    )
    image_part = pl.pallas_call(
        functools.partial(body, n, IMG_ROWS, spread_factor),
        out_shape=pltpu.VMEM((IMG_ROWS, 2, LANES), F32),
        in_specs=[pl.BlockSpec(memory_space=pltpu.HBM)] * len(operands),
        out_specs=pl.BlockSpec(memory_space=pltpu.VMEM),
        scratch_shapes=[pltpu.VMEM(x.shape, x.dtype) for x in operands]
        + [
            pltpu.VMEM((pulses, 2 * blocks + 2 * reach, LANES), F32),
            pltpu.VMEM((2, 8, count_tiles), F32),
            pltpu.VMEM((n, width, LANES), BF16),
            pltpu.VMEM((2, n, width, LANES), BF16),
            pltpu.VMEM((n, 1, LANES), F32),
            pltpu.VMEM((n, 1, LANES), F32),
            pltpu.VMEM((n, capacity, 2 * LANES), BF16),
            pltpu.VMEM((n, capacity, 2 * LANES), BF16),
            pltpu.VMEM((count_tiles, 2 * n * width), BF16),
            pltpu.VMEM((groups, 2 * rows, n * width), BF16),
            pltpu.VMEM((WEIGHTS, groups, rows, LANES), F32),
            pltpu.VMEM((groups, rows, LANES), jnp.int32),
            pltpu.VMEM((2, count_beams, n * width), F32),
            pltpu.SemaphoreType.DMA((9,)),
            pltpu.SemaphoreType.DMA((len(operands),)),
            pltpu.SemaphoreType.REGULAR,
        ],
        compiler_params=pltpu.CompilerParams(
            collective_id=0, has_side_effects=True, vmem_limit_bytes=62 << 20
        ),
    )(*operands)
    if pa > 1:
        image_part = lax.psum_scatter(image_part, "pa", scatter_dimension=0, tiled=True)
    return image_part[None]


def solution(mesh):
    placed = (
        P(("pa", "row"), None, None),
        P(),
        P("pa", None, None),
        P(None, "pa", None, "row"),
        P("pa", None, "row"),
        P("pa", None, "row"),
        P("pa", None, "row"),
        P("pa", None, "row"),
    )
    return jax.shard_map(
        functools.partial(per_device, mesh.shape["row"], mesh.shape["pa"]),
        mesh=mesh,
        in_specs=placed,
        out_specs=P("row", "pa", None, None),
        check_vma=False,
    )
```

```python
import functools

import jax
import jax.numpy as jnp
from jax import lax
from jax.experimental import pallas as pl
from jax.experimental.pallas import tpu as pltpu
from jax.sharding import PartitionSpec as P

LANES = 128
IMG_ROWS = 64
F32 = jnp.float32
BF16 = jnp.bfloat16
NT = (((1,), (1,)), ((), ()))
TN = (((0,), (0,)), ((), ()))
WEIGHTS = 4
LOW = (0, 2, 3, 1)
HIGH = (2, 3, 0, 1)
OUTER = (0, 1, 2, 3)
SCHEDULE = ((2, 2, 0, 0), (0, 0, 1, 1), (4, 3, 4, 4), (1, 7, 3, 2), (3, 4, 2, 3), (7, 1, 7, 7))


def iota(shape, dim):
    return lax.broadcasted_iota(jnp.int32, shape, dim)


def one_hot(cond):
    return jnp.where(cond, 1.0, 0.0)


def mirrored(me, n, i):
    if n & (n - 1):
        return lax.rem(me + i, n)
    return jnp.bitwise_xor(me, n - i)


def body(
    n,
    rows_out,
    scale,
    x_hbm,
    taps_hbm,
    angle_hbm,
    owner_hbm,
    slot_hbm,
    weight_hbm,
    phase_hbm,
    offset_hbm,
    out_ref,
    x_ref,
    taps_ref,
    angle_ref,
    owner_ref,
    slot_ref,
    weight_ref,
    phase_ref,
    offset_ref,
    xs,
    meta,
    send_one,
    recv_one,
    send_slot,
    recv_slot,
    send_two,
    recv_two,
    steer,
    packed,
    coeff,
    turn,
    turning,
    sems,
    load_sems,
    entered,
):
    me = lax.axis_index("row")
    pulses, blocks = x_ref.shape[0], x_ref.shape[1] // 2
    reach = taps_ref.shape[1] // LANES
    group = 2 * blocks // n
    width = pulses * group
    tiles = group // 2
    count_a, count_beams = angle_ref.shape
    count_tiles = tiles * count_beams
    capacity = send_two.shape[1]
    chunk = n // 4
    rows = chunk * capacity
    half = 2 * chunk
    side = lax.div(me, half)
    outer = jnp.logical_or(me < chunk, me >= n - chunk)
    mirror = jnp.where(side == 0, me + n - chunk, me - n + chunk)

    given = (x_hbm, taps_hbm, angle_hbm, owner_hbm, slot_hbm, weight_hbm, phase_hbm, offset_hbm)
    held = (x_ref, taps_ref, angle_ref, owner_ref, slot_ref, weight_ref, phase_ref, offset_ref)
    held_copies = [
        pltpu.make_async_copy(source, target, load_sems.at[index])
        for index, (source, target) in enumerate(zip(given, held))
    ]
    for copy in held_copies[:2]:
        copy.start()
    barrier = pltpu.get_barrier_semaphore()

    def greet(i, carry):
        to = (1 - side) * half + i
        pl.semaphore_signal(barrier, inc=1, device_id={"row": to})
        return carry

    lax.fori_loop(0, half, greet, 0)
    for copy in held_copies[2:]:
        copy.start()

    keep = iota((LANES, LANES), 1) >= iota((LANES, LANES), 0)
    zero = jnp.zeros((LANES, LANES), F32)
    held_copies[1].wait()
    halves = []
    for c in range(2):
        rolled = []
        for j in range(reach):
            row = taps_ref[c : c + 1, j * LANES : (j + 1) * LANES].astype(F32)
            row = jnp.broadcast_to(row, (LANES, LANES))
            rolled.append(pltpu.roll(row, 0, 1, stride=1, stride_axis=0))
        rolled = [zero] + rolled + [zero]
        halves.append(
            jnp.concatenate(
                [jnp.where(keep, rolled[j + 1], rolled[j]).astype(BF16) for j in range(reach + 1)], 1
            )
        )
    band = jnp.concatenate(halves, 0)

    for index in (3, 4, 5, 6, 7):
        held_copies[index].wait()
    weights = weight_ref[...].astype(F32)
    fields = [owner_ref[...].astype(F32), slot_ref[...].astype(F32)]
    fields += [weights[k] for k in range(WEIGHTS)]
    fields += [offset_ref[...].astype(F32), phase_ref[...].astype(F32)]
    meta[0] = jnp.concatenate(
        [jnp.concatenate([f[t : t + 1, :] for t in range(tiles)], 1) for f in fields], 0
    )

    held_copies[0].wait()
    for p in range(pulses):
        xs[p, : 2 * blocks, :] = x_ref[p].astype(F32)
        xs[p, 2 * blocks :, :] = jnp.zeros((2 * reach, LANES), F32)
    outs = []
    parity = iota((2 * blocks, LANES), 0) % 2 == 0
    for p in range(pulses):
        window = jnp.concatenate(
            [xs[p, 2 * j : 2 * j + 2 * blocks, :].astype(BF16) for j in range(reach + 1)], 1
        )
        product = lax.dot_general(window, band, NT, preferred_element_type=F32)
        first, second = product[:, :LANES], product[:, LANES:]
        crossed = jnp.where(
            parity, pltpu.roll(second, 2 * blocks - 1, 0), -pltpu.roll(second, 1, 0)
        )
        outs.append((first + crossed).reshape(n, group, LANES))
    send_one[...] = jnp.concatenate(outs, 1).astype(BF16)

    pl.semaphore_wait(barrier, half)
    plane_here, place_here = lax.div(me, chunk), lax.rem(me, chunk)

    @pl.when(jnp.logical_not(outer))
    def _():
        for plane in range(2):
            to = ((1 - side) * 2 + plane) * chunk + place_here
            pl.semaphore_signal(entered, inc=1, device_id={"row": to})


    def push(source, target, send_sem, recv_sem, to):
        pltpu.make_async_remote_copy(
            src_ref=source,
            dst_ref=target,
            send_sem=send_sem,
            recv_sem=recv_sem,
            device_id={"row": to},
        ).start()

    def keep_own(source, target, recv_sem):
        pltpu.make_async_copy(source, target, recv_sem).start()

    def exchange(source_of, target, send_sem, recv_sem):
        def first(i, carry):
            @pl.when(i != me)
            def _():
                push(source_of(i), target, send_sem, recv_sem, i)

            return carry

        def rest(i, carry):
            to = mirrored(me, n, i)

            @pl.when(to >= 2)
            def _():
                push(source_of(to), target, send_sem, recv_sem, to)

            return carry

        lax.fori_loop(0, 2, first, 0)
        lax.fori_loop(1, n, rest, 0)
        keep_own(source_of(me), target, recv_sem)

    def arrived(target, recv_sem):
        pltpu.make_async_copy(target, target, recv_sem).wait()

    departed = arrived

    @pl.when(outer)
    def _():
        push(meta.at[0], meta.at[1], sems.at[6], sems.at[7], mirror)

    def spread(plane, copy):
        shifted_plane = jnp.where(copy == 1, 3 - plane, plane)

        def one(i, carry):
            place = mirrored(place_here, chunk, i)
            to = plane * chunk + place
            source = send_one.at[shifted_plane * chunk + place]
            target = recv_one.at[copy, me]
            recv_sem = sems.at[1 + 7 * copy]

            @pl.when(to != me)
            def _():
                push(source, target, sems.at[0], recv_sem, to)

            @pl.when(to == me)
            def _():
                keep_own(source, target, recv_sem)

            return carry

        lax.fori_loop(1, chunk + 1, one, 0)

    for order, turn_of in enumerate(SCHEDULE):
        if order in (0, 3):

            @pl.when(side == (0 if order == 0 else 1))
            def _():
                pl.semaphore_wait(entered, 1)

        code = jnp.where(
            plane_here < 2,
            jnp.where(plane_here == 0, turn_of[0], turn_of[1]),
            jnp.where(plane_here == 2, turn_of[2], turn_of[3]),
        )
        spread(lax.rem(code, 4), lax.div(code, 4))

    before = one_hot(iota((count_tiles, count_tiles), 0) < iota((count_tiles, count_tiles), 1))
    before = before.astype(BF16)

    def ranked_tiles(known):
        owner = known[0:1].astype(jnp.int32)
        member = one_hot(owner == iota((n, count_tiles), 0))
        ahead = jnp.dot(member.astype(BF16), before, preferred_element_type=F32)
        rank = jnp.sum(ahead * member, 0, keepdims=True).astype(jnp.int32)
        return owner, member, rank

    known = meta[0]
    owner, member, rank = ranked_tiles(known)
    ranked = jnp.where(rank == iota((LANES, count_tiles), 0), known[1:2], 0.0)
    slots = lax.dot_general(
        member.astype(BF16), ranked.astype(BF16), NT, preferred_element_type=F32
    )
    send_slot[...] = slots.reshape(n, 1, LANES)

    held_copies[2].wait()
    span = n * width
    pulse_of = iota((count_a, span), 1) // group == iota((count_a, span), 0)
    expand = one_hot(pulse_of).astype(BF16)
    angles = angle_ref[...]
    cosine = lax.dot_general(
        jnp.cos(angles).astype(BF16), expand, TN, preferred_element_type=F32
    )
    sine = lax.dot_general(
        jnp.sin(angles).astype(BF16), expand, TN, preferred_element_type=F32
    )
    column = iota((count_beams, span), 1) % group
    even = column % 2 == 0
    turning[0] = jnp.where(even, cosine, -sine)
    turning[1] = jnp.where(even, sine, cosine)
    norm = count_a ** (-0.5)

    def prepare(known, owner, rank, begin, first, count):
        depth = count * rows
        near = lax.rem(owner + n - side * half, n) - begin
        place = near * capacity + rank
        pack = one_hot(place == iota((depth, count_tiles), 0)).astype(BF16)
        table = jnp.concatenate([known, jnp.zeros_like(known)], 0).astype(BF16)
        columns = lax.dot_general(pack, table, NT, preferred_element_type=F32)
        lane = iota((depth, LANES), 1)
        offset = jnp.broadcast_to(
            columns[:, 2 + WEIGHTS : 3 + WEIGHTS], (depth, LANES)
        ).astype(jnp.int32)
        turn[first : first + count] = (2 - offset).reshape(count, rows, LANES)
        for k in range(WEIGHTS):
            reached = lane + offset + (k - 1)
            inside = (reached >= 0) & (reached < LANES)
            level = jnp.where(inside, columns[:, 2 + k : 3 + k], 0.0)
            coeff[k, first : first + count] = level.reshape(count, rows, LANES)
        phases = known[3 + WEIGHTS : 4 + WEIGHTS]
        turns = [norm * jnp.cos(phases), norm * jnp.sin(phases)]
        turns = [
            f[:, t * count_beams : (t + 1) * count_beams] for f in turns for t in range(tiles)
        ]
        turns.append(jnp.zeros((LANES - 2 * tiles, count_beams), F32))
        turns = jnp.concatenate(turns, 0).T
        for t in range(tiles):
            here = column // 2 == t
            c = turns[:, t : t + 1]
            s = turns[:, tiles + t : tiles + t + 1]
            base = t * count_beams
            steer[base : base + count_beams, :span] = jnp.where(
                here, c * turning[0] - s * turning[1], 0.0
            ).astype(BF16)
            steer[base : base + count_beams, span:] = jnp.where(
                here, s * turning[0] + c * turning[1], 0.0
            ).astype(BF16)
        for j in range(count):
            part = jnp.dot(
                pack[j * rows : (j + 1) * rows], steer[...], preferred_element_type=F32
            ).astype(BF16)
            packed[first + j, :rows, :] = part[:, :span]
            packed[first + j, rows:, :] = part[:, span:]

    def form(turned, entry, begin, block):
        formed = jnp.dot(packed[entry], turned, preferred_element_type=F32)
        by = turn[entry]
        one, two, four = (by & 1) == 1, (by & 2) == 2, by >= 4
        taps = [coeff[k, entry] for k in range(WEIGHTS)]
        shifted = []
        for c in range(2):
            x = formed[c * rows : (c + 1) * rows]
            x = jnp.where(one, x, pltpu.roll(x, LANES - 1, 1))
            x = jnp.where(two, pltpu.roll(x, 2, 1), x)
            x = jnp.where(four, pltpu.roll(x, 4, 1), x)
            total = taps[0] * x
            for k in range(1, WEIGHTS):
                total = total + taps[k] * pltpu.roll(x, LANES - k, 1)
            shifted.append(total)
        ready = jnp.concatenate(shifted, 1).astype(BF16)
        at = entry * chunk
        send_two[pl.ds(at, chunk)] = ready.reshape(chunk, capacity, 2 * LANES)

        def give(step, carry):
            pair = lax.div(step, 2)
            swap = jnp.where(pair == 1, 2, jnp.where(pair == 2, -2, 0)) if chunk == 8 else 0
            i = step + swap
            to = lax.rem(begin + i + side * half, n)

            @pl.when(to != me)
            def _():
                push(send_two.at[at + i], recv_two.at[block], sems.at[4], sems.at[5], to)

            @pl.when(to == me)
            def _():
                keep_own(send_two.at[at + i], recv_two.at[block], sems.at[5])

            return carry

        lax.fori_loop(0, chunk, give, 0, unroll=True)

    prepare(known, owner, rank, 0, 0, 2)

    @pl.when(outer)
    def _():
        arrived(meta.at[1], sems.at[7])

    other = jnp.where(outer, 1, 0)
    known = meta[other]
    owner, member, rank = ranked_tiles(known)
    begin = jnp.where(outer, 0, half)
    prepare(known, owner, rank, begin, 2, 2)
    exchange(lambda to: send_slot.at[to], recv_slot.at[me], sems.at[2], sems.at[3])
    arrived(recv_one.at[0], sems.at[1])
    for step in range(4):
        if step == OUTER.index(2):

            @pl.when(outer)
            def _():
                arrived(recv_one.at[1], sems.at[8])

        entry = jnp.where(outer, OUTER[step], jnp.where(side == 0, LOW[step], HIGH[step]))
        late = lax.div(entry, 2)
        moved = late * other
        turned = recv_one[moved].reshape(span, LANES)
        form(
            turned,
            entry,
            lax.rem(entry, 2) * chunk + late * begin,
            jnp.where(moved == 1, mirror, me),
        )

    arrived(recv_slot, sems.at[3])
    total_slots = n * capacity
    got = recv_slot[...].reshape(n, LANES).astype(BF16)
    source_of = iota((total_slots, n), 0) // capacity == iota((total_slots, n), 1)
    got = jnp.dot(one_hot(source_of).astype(BF16), got, preferred_element_type=F32)
    wanted = iota((total_slots, LANES), 0) % capacity == iota((total_slots, LANES), 1)
    got = jnp.sum(jnp.where(wanted, got, 0.0), 1, keepdims=True).astype(jnp.int32)
    select = one_hot(got == iota((total_slots, LANES), 1)).T[:rows_out].astype(BF16)
    arrived(recv_two, sems.at[5])
    landed = recv_two[...].reshape(total_slots, 2 * LANES)
    image = jnp.dot(select, landed, preferred_element_type=F32) * scale
    out_ref[:, 0, :] = image[:, :LANES]
    out_ref[:, 1, :] = image[:, LANES:]
    departed(send_slot.at[pl.ds(0, n - 1)], sems.at[2])
    departed(recv_one.at[0, pl.ds(0, n - 1)], sems.at[0])

    @pl.when(outer)
    def _():
        departed(meta.at[0], sems.at[6])
        departed(recv_one.at[0, pl.ds(0, 2 * chunk - 1)], sems.at[0])
        departed(send_two.at[pl.ds(0, n - 2)], sems.at[4])

    @pl.when(jnp.logical_not(outer))
    def _():
        departed(recv_one.at[0, pl.ds(0, 2 * chunk)], sems.at[0])
        departed(send_two.at[pl.ds(0, n - 1)], sems.at[4])


def per_device(
    n,
    pa,
    raw_pulses,
    chirp_taps,
    steer_angle,
    interp_weights,
    tile_phase,
    tap_offset,
    image_slot,
    tile_owner,
):
    pulses, _, length = raw_pulses.shape
    _, count_a, count_beams = steer_angle.shape
    tiles = tile_owner.shape[2]
    count_tiles = count_beams * tiles
    capacity = 2 * count_tiles // n
    groups, chunk = 4, n // 4
    rows = chunk * capacity
    blocks = length // LANES
    width = pulses * 2 * blocks // n
    reach = chirp_taps.shape[1] // LANES
    spread_factor = float(pa * count_tiles // IMG_ROWS) ** (-0.5)
    lines = raw_pulses.reshape(pulses, 2, blocks, LANES).transpose(0, 2, 1, 3)
    operands = (
        lines.reshape(pulses, 2 * blocks, LANES),
        chirp_taps,
        steer_angle.reshape(count_a, count_beams),
        tile_owner.transpose(0, 2, 1).reshape(tiles, count_beams),
        image_slot.transpose(0, 2, 1).reshape(tiles, count_beams),
        interp_weights.transpose(0, 1, 3, 2).reshape(4, tiles, count_beams),
        tile_phase.transpose(0, 2, 1).reshape(tiles, count_beams),
        tap_offset.transpose(0, 2, 1).reshape(tiles, count_beams),
    )
    image_part = pl.pallas_call(
        functools.partial(body, n, IMG_ROWS, spread_factor),
        out_shape=pltpu.VMEM((IMG_ROWS, 2, LANES), F32),
        in_specs=[pl.BlockSpec(memory_space=pltpu.HBM)] * len(operands),
        out_specs=pl.BlockSpec(memory_space=pltpu.VMEM),
        scratch_shapes=[pltpu.VMEM(x.shape, x.dtype) for x in operands]
        + [
            pltpu.VMEM((pulses, 2 * blocks + 2 * reach, LANES), F32),
            pltpu.VMEM((2, 8, count_tiles), F32),
            pltpu.VMEM((n, width, LANES), BF16),
            pltpu.VMEM((2, n, width, LANES), BF16),
            pltpu.VMEM((n, 1, LANES), F32),
            pltpu.VMEM((n, 1, LANES), F32),
            pltpu.VMEM((n, capacity, 2 * LANES), BF16),
            pltpu.VMEM((n, capacity, 2 * LANES), BF16),
            pltpu.VMEM((count_tiles, 2 * n * width), BF16),
            pltpu.VMEM((groups, 2 * rows, n * width), BF16),
            pltpu.VMEM((WEIGHTS, groups, rows, LANES), F32),
            pltpu.VMEM((groups, rows, LANES), jnp.int32),
            pltpu.VMEM((2, count_beams, n * width), F32),
            pltpu.SemaphoreType.DMA((9,)),
            pltpu.SemaphoreType.DMA((len(operands),)),
            pltpu.SemaphoreType.REGULAR,
        ],
        compiler_params=pltpu.CompilerParams(
            collective_id=0, has_side_effects=True, vmem_limit_bytes=62 << 20
        ),
    )(*operands)
    if pa > 1:
        image_part = lax.psum_scatter(image_part, "pa", scatter_dimension=0, tiled=True)
    return image_part[None]


def solution(mesh):
    placed = (
        P(("pa", "row"), None, None),
        P(),
        P("pa", None, None),
        P(None, "pa", None, "row"),
        P("pa", None, "row"),
        P("pa", None, "row"),
        P("pa", None, "row"),
        P("pa", None, "row"),
    )
    return jax.shard_map(
        functools.partial(per_device, mesh.shape["row"], mesh.shape["pa"]),
        mesh=mesh,
        in_specs=placed,
        out_specs=P("row", "pa", None, None),
        check_vma=False,
    )
```

```python
import functools

import jax
import jax.numpy as jnp
from jax import lax
from jax.experimental import pallas as pl
from jax.experimental.pallas import tpu as pltpu
from jax.sharding import PartitionSpec as P

LANES = 128
IMG_ROWS = 64
F32 = jnp.float32
BF16 = jnp.bfloat16
NT = (((1,), (1,)), ((), ()))
TN = (((0,), (0,)), ((), ()))
WEIGHTS = 4
LOW = (0, 2, 3, 1)
HIGH = (2, 3, 0, 1)
OUTER = (0, 1, 2, 3)
SCHEDULE = ((2, 2, 0, 0), (0, 0, 1, 1), (4, 3, 4, 4), (1, 7, 3, 2), (3, 4, 2, 3), (7, 1, 7, 7))


def iota(shape, dim):
    return lax.broadcasted_iota(jnp.int32, shape, dim)


def one_hot(cond):
    return jnp.where(cond, 1.0, 0.0)


def mirrored(me, n, i):
    if n & (n - 1):
        return lax.rem(me + i, n)
    return jnp.bitwise_xor(me, n - i)


def body(
    n,
    rows_out,
    scale,
    x_hbm,
    taps_hbm,
    angle_hbm,
    owner_hbm,
    slot_hbm,
    weight_hbm,
    phase_hbm,
    offset_hbm,
    out_ref,
    x_ref,
    taps_ref,
    angle_ref,
    owner_ref,
    slot_ref,
    weight_ref,
    phase_ref,
    offset_ref,
    xs,
    meta,
    send_one,
    recv_one,
    send_slot,
    recv_slot,
    send_two,
    recv_two,
    steer,
    packed,
    coeff,
    turn,
    turning,
    chosen,
    sems,
    load_sems,
    entered,
):
    me = lax.axis_index("row")
    pulses, blocks = x_ref.shape[0], x_ref.shape[1] // 2
    reach = taps_ref.shape[1] // LANES
    group = 2 * blocks // n
    width = pulses * group
    tiles = group // 2
    count_a, count_beams = angle_ref.shape
    count_tiles = tiles * count_beams
    capacity = send_two.shape[1]
    chunk = n // 4
    rows = chunk * capacity
    half = 2 * chunk
    side = lax.div(me, half)
    outer = jnp.logical_or(me < chunk, me >= n - chunk)
    mirror = jnp.where(side == 0, me + n - chunk, me - n + chunk)

    given = (x_hbm, taps_hbm, angle_hbm, owner_hbm, slot_hbm, weight_hbm, phase_hbm, offset_hbm)
    held = (x_ref, taps_ref, angle_ref, owner_ref, slot_ref, weight_ref, phase_ref, offset_ref)
    held_copies = [
        pltpu.make_async_copy(source, target, load_sems.at[index])
        for index, (source, target) in enumerate(zip(given, held))
    ]
    for copy in held_copies[:2]:
        copy.start()
    barrier = pltpu.get_barrier_semaphore()

    def greet(i, carry):
        to = (1 - side) * half + i
        pl.semaphore_signal(barrier, inc=1, device_id={"row": to})
        return carry

    lax.fori_loop(0, half, greet, 0)
    for copy in held_copies[2:]:
        copy.start()

    keep = iota((LANES, LANES), 1) >= iota((LANES, LANES), 0)
    zero = jnp.zeros((LANES, LANES), F32)
    held_copies[1].wait()
    halves = []
    for c in range(2):
        rolled = []
        for j in range(reach):
            row = taps_ref[c : c + 1, j * LANES : (j + 1) * LANES].astype(F32)
            row = jnp.broadcast_to(row, (LANES, LANES))
            rolled.append(pltpu.roll(row, 0, 1, stride=1, stride_axis=0))
        rolled = [zero] + rolled + [zero]
        halves.append(
            jnp.concatenate(
                [jnp.where(keep, rolled[j + 1], rolled[j]).astype(BF16) for j in range(reach + 1)], 1
            )
        )
    band = jnp.concatenate(halves, 0)

    for index in (3, 4, 5, 6, 7):
        held_copies[index].wait()
    weights = weight_ref[...].astype(F32)
    fields = [owner_ref[...].astype(F32), slot_ref[...].astype(F32)]
    fields += [weights[k] for k in range(WEIGHTS)]
    fields += [offset_ref[...].astype(F32), phase_ref[...].astype(F32)]
    meta[0] = jnp.concatenate(
        [jnp.concatenate([f[t : t + 1, :] for t in range(tiles)], 1) for f in fields], 0
    )

    held_copies[0].wait()
    for p in range(pulses):
        xs[p, : 2 * blocks, :] = x_ref[p].astype(F32)
        xs[p, 2 * blocks :, :] = jnp.zeros((2 * reach, LANES), F32)
    outs = []
    parity = iota((2 * blocks, LANES), 0) % 2 == 0
    for p in range(pulses):
        window = jnp.concatenate(
            [xs[p, 2 * j : 2 * j + 2 * blocks, :].astype(BF16) for j in range(reach + 1)], 1
        )
        product = lax.dot_general(window, band, NT, preferred_element_type=F32)
        first, second = product[:, :LANES], product[:, LANES:]
        crossed = jnp.where(
            parity, pltpu.roll(second, 2 * blocks - 1, 0), -pltpu.roll(second, 1, 0)
        )
        outs.append((first + crossed).reshape(n, group, LANES))
    send_one[...] = jnp.concatenate(outs, 1).astype(BF16)

    pl.semaphore_wait(barrier, half)
    plane_here, place_here = lax.div(me, chunk), lax.rem(me, chunk)

    @pl.when(jnp.logical_not(outer))
    def _():
        for plane in range(2):
            to = ((1 - side) * 2 + plane) * chunk + place_here
            pl.semaphore_signal(entered, inc=1, device_id={"row": to})


    def push(source, target, send_sem, recv_sem, to):
        pltpu.make_async_remote_copy(
            src_ref=source,
            dst_ref=target,
            send_sem=send_sem,
            recv_sem=recv_sem,
            device_id={"row": to},
        ).start()

    def keep_own(source, target, recv_sem):
        pltpu.make_async_copy(source, target, recv_sem).start()

    def exchange(source_of, target, send_sem, recv_sem):
        def first(i, carry):
            @pl.when(i != me)
            def _():
                push(source_of(i), target, send_sem, recv_sem, i)

            return carry

        def rest(i, carry):
            to = mirrored(me, n, i)

            @pl.when(to >= 2)
            def _():
                push(source_of(to), target, send_sem, recv_sem, to)

            return carry

        lax.fori_loop(0, 2, first, 0)
        lax.fori_loop(1, n, rest, 0)
        keep_own(source_of(me), target, recv_sem)

    def arrived(target, recv_sem):
        pltpu.make_async_copy(target, target, recv_sem).wait()

    departed = arrived

    @pl.when(outer)
    def _():
        push(meta.at[0], meta.at[1], sems.at[6], sems.at[7], mirror)

    def spread(plane, copy):
        shifted_plane = jnp.where(copy == 1, 3 - plane, plane)

        def one(i, carry):
            place = mirrored(place_here, chunk, i)
            to = plane * chunk + place
            source = send_one.at[shifted_plane * chunk + place]
            target = recv_one.at[copy, me]
            recv_sem = sems.at[1 + 7 * copy]

            @pl.when(to != me)
            def _():
                push(source, target, sems.at[0], recv_sem, to)

            @pl.when(to == me)
            def _():
                keep_own(source, target, recv_sem)

            return carry

        lax.fori_loop(1, chunk + 1, one, 0)

    for order, turn_of in enumerate(SCHEDULE):
        if order in (0, 3):

            @pl.when(side == (0 if order == 0 else 1))
            def _():
                pl.semaphore_wait(entered, 1)

        code = jnp.where(
            plane_here < 2,
            jnp.where(plane_here == 0, turn_of[0], turn_of[1]),
            jnp.where(plane_here == 2, turn_of[2], turn_of[3]),
        )
        spread(lax.rem(code, 4), lax.div(code, 4))

    before = one_hot(iota((count_tiles, count_tiles), 0) < iota((count_tiles, count_tiles), 1))
    before = before.astype(BF16)

    def ranked_tiles(known):
        owner = known[0:1].astype(jnp.int32)
        member = one_hot(owner == iota((n, count_tiles), 0))
        ahead = jnp.dot(member.astype(BF16), before, preferred_element_type=F32)
        rank = jnp.sum(ahead * member, 0, keepdims=True).astype(jnp.int32)
        return owner, member, rank

    known = meta[0]
    owner, member, rank = ranked_tiles(known)
    ranked = jnp.where(rank == iota((LANES, count_tiles), 0), known[1:2], 0.0)
    slots = lax.dot_general(
        member.astype(BF16), ranked.astype(BF16), NT, preferred_element_type=F32
    )
    send_slot[...] = slots.reshape(n, 1, LANES)

    held_copies[2].wait()
    span = n * width
    pulse_of = iota((count_a, span), 1) // group == iota((count_a, span), 0)
    expand = one_hot(pulse_of).astype(BF16)
    angles = angle_ref[...]
    cosine = lax.dot_general(
        jnp.cos(angles).astype(BF16), expand, TN, preferred_element_type=F32
    )
    sine = lax.dot_general(
        jnp.sin(angles).astype(BF16), expand, TN, preferred_element_type=F32
    )
    column = iota((count_beams, span), 1) % group
    even = column % 2 == 0
    turning[0] = jnp.where(even, cosine, -sine)
    turning[1] = jnp.where(even, sine, cosine)
    norm = count_a ** (-0.5)

    def prepare(known, owner, rank, begin, first, count):
        depth = count * rows
        near = lax.rem(owner + n - side * half, n) - begin
        place = near * capacity + rank
        pack = one_hot(place == iota((depth, count_tiles), 0)).astype(BF16)
        table = jnp.concatenate([known, jnp.zeros_like(known)], 0).astype(BF16)
        columns = lax.dot_general(pack, table, NT, preferred_element_type=F32)
        lane = iota((depth, LANES), 1)
        offset = jnp.broadcast_to(
            columns[:, 2 + WEIGHTS : 3 + WEIGHTS], (depth, LANES)
        ).astype(jnp.int32)
        turn[first : first + count] = (2 - offset).reshape(count, rows, LANES)
        for k in range(WEIGHTS):
            reached = lane + offset + (k - 1)
            inside = (reached >= 0) & (reached < LANES)
            level = jnp.where(inside, columns[:, 2 + k : 3 + k], 0.0)
            coeff[k, first : first + count] = level.reshape(count, rows, LANES)
        phases = known[3 + WEIGHTS : 4 + WEIGHTS]
        turns = [norm * jnp.cos(phases), norm * jnp.sin(phases)]
        turns = [
            f[:, t * count_beams : (t + 1) * count_beams] for f in turns for t in range(tiles)
        ]
        turns.append(jnp.zeros((LANES - 2 * tiles, count_beams), F32))
        turns = jnp.concatenate(turns, 0).T
        for t in range(tiles):
            here = column // 2 == t
            c = turns[:, t : t + 1]
            s = turns[:, tiles + t : tiles + t + 1]
            base = t * count_beams
            steer[base : base + count_beams, :span] = jnp.where(
                here, c * turning[0] - s * turning[1], 0.0
            ).astype(BF16)
            steer[base : base + count_beams, span:] = jnp.where(
                here, s * turning[0] + c * turning[1], 0.0
            ).astype(BF16)
        for j in range(count):
            part = jnp.dot(
                pack[j * rows : (j + 1) * rows], steer[...], preferred_element_type=F32
            ).astype(BF16)
            packed[first + j, :rows, :] = part[:, :span]
            packed[first + j, rows:, :] = part[:, span:]

    def form(turned, entry, begin, block):
        formed = jnp.dot(packed[entry], turned, preferred_element_type=F32)
        by = turn[entry]
        one, two, four = (by & 1) == 1, (by & 2) == 2, by >= 4
        taps = [coeff[k, entry] for k in range(WEIGHTS)]
        shifted = []
        for c in range(2):
            x = formed[c * rows : (c + 1) * rows]
            x = jnp.where(one, x, pltpu.roll(x, LANES - 1, 1))
            x = jnp.where(two, pltpu.roll(x, 2, 1), x)
            x = jnp.where(four, pltpu.roll(x, 4, 1), x)
            total = taps[0] * x
            for k in range(1, WEIGHTS):
                total = total + taps[k] * pltpu.roll(x, LANES - k, 1)
            shifted.append(total)
        ready = jnp.concatenate(shifted, 1).astype(BF16)
        at = entry * chunk
        recv_sem = sems.at[9 + lax.div(block, chunk)]
        send_two[pl.ds(at, chunk)] = ready.reshape(chunk, capacity, 2 * LANES)

        def give(step, carry):
            pair = lax.div(step, 2)
            swap = jnp.where(pair == 1, 2, jnp.where(pair == 2, -2, 0)) if chunk == 8 else 0
            i = step + swap
            to = lax.rem(begin + i + side * half, n)

            @pl.when(to != me)
            def _():
                push(send_two.at[at + i], recv_two.at[block], sems.at[4], recv_sem, to)

            @pl.when(to == me)
            def _():
                keep_own(send_two.at[at + i], recv_two.at[block], recv_sem)

            return carry

        lax.fori_loop(0, chunk, give, 0, unroll=True)

    prepare(known, owner, rank, 0, 0, 2)

    @pl.when(outer)
    def _():
        arrived(meta.at[1], sems.at[7])

    other = jnp.where(outer, 1, 0)
    known = meta[other]
    owner, member, rank = ranked_tiles(known)
    begin = jnp.where(outer, 0, half)
    prepare(known, owner, rank, begin, 2, 2)
    exchange(lambda to: send_slot.at[to], recv_slot.at[me], sems.at[2], sems.at[3])
    arrived(recv_one.at[0], sems.at[1])
    for step in range(4):
        if step == OUTER.index(2):

            @pl.when(outer)
            def _():
                arrived(recv_one.at[1], sems.at[8])

        entry = jnp.where(outer, OUTER[step], jnp.where(side == 0, LOW[step], HIGH[step]))
        late = lax.div(entry, 2)
        moved = late * other
        turned = recv_one[moved].reshape(span, LANES)
        form(
            turned,
            entry,
            lax.rem(entry, 2) * chunk + late * begin,
            jnp.where(moved == 1, mirror, me),
        )

    arrived(recv_slot, sems.at[3])
    total_slots = n * capacity
    got = recv_slot[...].reshape(n, LANES).astype(BF16)
    source_of = iota((total_slots, n), 0) // capacity == iota((total_slots, n), 1)
    got = jnp.dot(one_hot(source_of).astype(BF16), got, preferred_element_type=F32)
    wanted = iota((total_slots, LANES), 0) % capacity == iota((total_slots, LANES), 1)
    got = jnp.sum(jnp.where(wanted, got, 0.0), 1, keepdims=True).astype(jnp.int32)
    select = one_hot(got == iota((total_slots, LANES), 1)).T[:rows_out].astype(BF16)
    for plane in range(4):
        chosen[plane] = select[:, plane * rows : (plane + 1) * rows]
    image = jnp.zeros((select.shape[0], 2 * LANES), F32)
    for low, high in ((1, 2), (2, 1), (0, 3), (3, 0)):
        plane = jnp.where(side == 0, low, high)
        landed = recv_two.at[pl.ds(plane * chunk, chunk)]
        arrived(landed, sems.at[9 + plane])
        image = image + jnp.dot(
            chosen[plane],
            landed[...].reshape(rows, 2 * LANES),
            preferred_element_type=F32,
        )
    image = image * scale
    out_ref[:, 0, :] = image[:, :LANES]
    out_ref[:, 1, :] = image[:, LANES:]
    departed(send_slot.at[pl.ds(0, n - 1)], sems.at[2])
    departed(recv_one.at[0, pl.ds(0, n - 1)], sems.at[0])

    @pl.when(outer)
    def _():
        departed(meta.at[0], sems.at[6])
        departed(recv_one.at[0, pl.ds(0, 2 * chunk - 1)], sems.at[0])
        departed(send_two.at[pl.ds(0, n - 2)], sems.at[4])

    @pl.when(jnp.logical_not(outer))
    def _():
        departed(recv_one.at[0, pl.ds(0, 2 * chunk)], sems.at[0])
        departed(send_two.at[pl.ds(0, n - 1)], sems.at[4])


def per_device(
    n,
    pa,
    raw_pulses,
    chirp_taps,
    steer_angle,
    interp_weights,
    tile_phase,
    tap_offset,
    image_slot,
    tile_owner,
):
    pulses, _, length = raw_pulses.shape
    _, count_a, count_beams = steer_angle.shape
    tiles = tile_owner.shape[2]
    count_tiles = count_beams * tiles
    capacity = 2 * count_tiles // n
    groups, chunk = 4, n // 4
    rows = chunk * capacity
    blocks = length // LANES
    width = pulses * 2 * blocks // n
    reach = chirp_taps.shape[1] // LANES
    spread_factor = float(pa * count_tiles // IMG_ROWS) ** (-0.5)
    lines = raw_pulses.reshape(pulses, 2, blocks, LANES).transpose(0, 2, 1, 3)
    operands = (
        lines.reshape(pulses, 2 * blocks, LANES),
        chirp_taps,
        steer_angle.reshape(count_a, count_beams),
        tile_owner.transpose(0, 2, 1).reshape(tiles, count_beams),
        image_slot.transpose(0, 2, 1).reshape(tiles, count_beams),
        interp_weights.transpose(0, 1, 3, 2).reshape(4, tiles, count_beams),
        tile_phase.transpose(0, 2, 1).reshape(tiles, count_beams),
        tap_offset.transpose(0, 2, 1).reshape(tiles, count_beams),
    )
    image_part = pl.pallas_call(
        functools.partial(body, n, IMG_ROWS, spread_factor),
        out_shape=pltpu.VMEM((IMG_ROWS, 2, LANES), F32),
        in_specs=[pl.BlockSpec(memory_space=pltpu.HBM)] * len(operands),
        out_specs=pl.BlockSpec(memory_space=pltpu.VMEM),
        scratch_shapes=[pltpu.VMEM(x.shape, x.dtype) for x in operands]
        + [
            pltpu.VMEM((pulses, 2 * blocks + 2 * reach, LANES), F32),
            pltpu.VMEM((2, 8, count_tiles), F32),
            pltpu.VMEM((n, width, LANES), BF16),
            pltpu.VMEM((2, n, width, LANES), BF16),
            pltpu.VMEM((n, 1, LANES), F32),
            pltpu.VMEM((n, 1, LANES), F32),
            pltpu.VMEM((n, capacity, 2 * LANES), BF16),
            pltpu.VMEM((n, capacity, 2 * LANES), BF16),
            pltpu.VMEM((count_tiles, 2 * n * width), BF16),
            pltpu.VMEM((groups, 2 * rows, n * width), BF16),
            pltpu.VMEM((WEIGHTS, groups, rows, LANES), F32),
            pltpu.VMEM((groups, rows, LANES), jnp.int32),
            pltpu.VMEM((2, count_beams, n * width), F32),
            pltpu.VMEM((4, IMG_ROWS, rows), BF16),
            pltpu.SemaphoreType.DMA((13,)),
            pltpu.SemaphoreType.DMA((len(operands),)),
            pltpu.SemaphoreType.REGULAR,
        ],
        compiler_params=pltpu.CompilerParams(
            collective_id=0, has_side_effects=True, vmem_limit_bytes=62 << 20
        ),
    )(*operands)
    if pa > 1:
        image_part = lax.psum_scatter(image_part, "pa", scatter_dimension=0, tiled=True)
    return image_part[None]


def solution(mesh):
    placed = (
        P(("pa", "row"), None, None),
        P(),
        P("pa", None, None),
        P(None, "pa", None, "row"),
        P("pa", None, "row"),
        P("pa", None, "row"),
        P("pa", None, "row"),
        P("pa", None, "row"),
    )
    return jax.shard_map(
        functools.partial(per_device, mesh.shape["row"], mesh.shape["pa"]),
        mesh=mesh,
        in_specs=placed,
        out_specs=P("row", "pa", None, None),
        check_vma=False,
    )
```
